32 devices in a mesh: groups: 2 (over y), space: 4 (over z), tm: 2 (over x), chan: 2 (over core).
Axes of the slice: x: 2, y: 2, z: 4, core: 2. Of those that a mesh axis runs over, the one named last changes fastest.
Arguments:
- features: float32 [48, 40, 384], P(('groups', 'space'), 'tm'), parts along dimension 0, may hold values from -50 to 50
- norm1_gain: float32 [384], replicated, may hold values from 0.25 to 1.75
- norm1_shift: float32 [384], replicated, may hold values from -3 to 3
- conv1_weight: float32 [3, 3, 384, 384], P(None, None, 'space', 'chan'), may hold values from -0.109375 to 0.109375
- norm2_gain: float32 [384], replicated, may hold values from 0.25 to 1.75
- norm2_shift: float32 [384], replicated, may hold values from -3 to 3
- conv2_weight: float32 [3, 3, 384, 384], P(None, None, 'space', 'chan'), may hold values from -0.109375 to 0.109375
- head_gain: float32 [384], replicated, may hold values from 0.25 to 1.75
- head_shift: float32 [384], replicated, may hold values from -3 to 3
- head_weight: float32 [3, 3, 384, 16], P(None, None, 'space', 'chan'), may hold values from -0.109375 to 0.109375
- head_bias: float32 [16], P('chan'), may hold values from -3 to 3
- noisy_latents: float32 [4, 16, 24, 40], P(('groups', 'tm'), None, 'space'), parts along dimension 0, may hold values from -6 to 6
- later_cond: float32 [4, 16, 24, 40], P(('groups', 'tm'), None, 'space'), parts along dimension 0, may hold values from -6 to 6
- patch_weight: float32 [144, 5120], P(None, 'chan'), may hold values from -0.5 to 0.5
- patch_bias: float32 [5120], P('chan'), may hold values from -3 to 3
Outputs:
- tokens: float32 [4, 12, 20, 5120], P(('groups', 'tm'), 'space', None, 'chan'), parts along dimension 0
- image_latent: float32 [48, 40, 16], P(('groups', 'space'), 'tm'), parts along dimension 0
The draws below stay inside these ranges and needn't reach their ends.
There are 2 independent parts, one for each index of `groups`. The reference program is written for one: setup_inputs(seed, part) draws one part's arguments, and reference() takes and returns one part's arrays. A program takes and returns all parts, laid end to end along the dimension named above; an argument that names none is the same for every part. Nothing has to cross between parts.
All inputs are finite; a program needn't handle non-finite values.
Results may differ from the reference program's by a relative error of at most 0.00007.
Values sent between devices are 32-bit elements; how exact they have to be, the bound alone decides.
A program may use at most 64 MiB of HBM per device.

```python
import math
import jax
import jax.numpy as jnp
from jax import lax

CH = 384
NGROUP = 32
ZDIM = 16
DIM = 5120
LAT_H = 24
LAT_W = 40
FRAMES = 2
PATCH_IN = 144


def draw_features(key, part):
    subkeys = jax.random.split(key, 4)
    row_pos = jnp.arange(LAT_H, dtype=jnp.float32) / (LAT_H - 1)
    row_ramp = 3.0 ** row_pos
    column_scale = jax.random.uniform(subkeys[0], (LAT_W,), minval=0.7, maxval=1.3)
    offsets = jax.random.uniform(subkeys[1], (CH,), minval=-1.0, maxval=1.0)
    random_part = jax.random.truncated_normal(subkeys[2], -4.0, 4.0, (LAT_H, LAT_W, CH))
    amplitude = jnp.exp(jax.random.uniform(subkeys[3], (CH,), minval=math.log(0.5), maxval=math.log(1.5)))
    return offsets + amplitude * row_ramp[:, None, None] * column_scale[None, :, None] * random_part


def shard_levels(own_key, extent, pieces, least, high):
    def one(position, blocks):
        draws = jax.random.uniform(jax.random.fold_in(jax.random.fold_in(own_key, 6), position), (blocks,), jnp.float32, least / len(pieces), high / len(pieces))
        return jnp.repeat(jnp.exp(draws), extent[position] // blocks).reshape((-1,) + (1,) * (len(extent) - position - 1))

    level = one(*pieces[0])
    for cut in pieces[1:]:
        level = level * one(*cut)
    return level


def centred(key, extent, deviation, most, pieces=(), kind=jnp.bfloat16):
    level = shard_levels(key, extent, pieces, -0.22, 0.18) if pieces else 1.0
    values = jax.random.normal(key, extent, jnp.float32) * deviation * level
    return jnp.minimum(jnp.maximum(values, -most), most).astype(kind)


def setup_inputs(seed: int = 0, part: int = 0) -> dict:
    key_list = jax.random.split(jax.random.key(seed), 16)
    own_keys = jax.random.split(jax.random.fold_in(key_list[15], part), 16)
    return {
        "features": draw_features(jax.random.fold_in(jax.random.fold_in(key_list[15], part), 71), part),
        "norm1_gain": jnp.clip(1.0 + 0.15 * jax.random.normal(key_list[1], (CH,), jnp.float32), 0.25, 1.75),
        "norm1_shift": centred(key_list[2], (CH,), 0.5, 3.0, (), jnp.float32),
        "conv1_weight": centred(key_list[3], (3, 3, CH, CH), (9 * CH) ** -0.5, 0.109375, ((2, 4), (3, 2)), jnp.float32),
        "norm2_gain": jnp.clip(1.0 + 0.15 * jax.random.normal(key_list[4], (CH,), jnp.float32), 0.25, 1.75),
        "norm2_shift": centred(key_list[5], (CH,), 0.5, 3.0, (), jnp.float32),
        "conv2_weight": centred(key_list[6], (3, 3, CH, CH), (9 * CH) ** -0.5, 0.109375, ((2, 4), (3, 2)), jnp.float32),
        "head_gain": jnp.clip(1.0 + 0.15 * jax.random.normal(key_list[7], (CH,), jnp.float32), 0.25, 1.75),
        "head_shift": centred(key_list[8], (CH,), 0.5, 3.0, (), jnp.float32),
        "head_weight": centred(key_list[9], (3, 3, CH, ZDIM), (9 * CH) ** -0.5, 0.109375, ((2, 4), (3, 2)), jnp.float32),
        "head_bias": centred(key_list[10], (ZDIM,), 0.5, 3.0, ((0, 2),), jnp.float32),
        "noisy_latents": centred(own_keys[11], (FRAMES, ZDIM, LAT_H, LAT_W), 1.0, 6.0, ((0, 2), (2, 4)), jnp.float32),
        "later_cond": centred(own_keys[12], (FRAMES, ZDIM, LAT_H, LAT_W), 1.0, 6.0, ((0, 2), (2, 4)), jnp.float32),
        "patch_weight": centred(key_list[13], (PATCH_IN, DIM), PATCH_IN ** -0.5, 0.5, ((1, 2),), jnp.float32),
        "patch_bias": centred(key_list[14], (DIM,), 0.5, 3.0, ((0, 2),), jnp.float32),
    }


EPSILON = 1e-06

def group_norm_act(values, gain, shift):
    height, width, depth = values.shape
    grouped = values.reshape(height * width, NGROUP, depth // NGROUP)
    center = lax.optimization_barrier(jnp.mean(grouped, axis=(0, 2), keepdims=True))
    spread = lax.optimization_barrier(jnp.mean(jnp.square(grouped - center), axis=(0, 2), keepdims=True))
    scaled = ((grouped - center) * lax.rsqrt(spread + EPSILON)).reshape(height, width, depth)
    return jax.nn.silu(scaled * gain + shift)

def conv_three(values, weight):
    result = lax.conv_general_dilated(values[None], weight, (1, 1), ((1, 1), (1, 1)), dimension_numbers=('NHWC', 'HWIO', 'NHWC'), precision=lax.Precision.HIGHEST)
    return result[0]

def reference(features, norm1_gain, norm1_shift, conv1_weight, norm2_gain, norm2_shift, conv2_weight, head_gain, head_shift, head_weight, head_bias, noisy_latents, later_cond, patch_weight, patch_bias):
    first_conv = conv_three(group_norm_act(features, norm1_gain, norm1_shift), conv1_weight)
    hidden = features + conv_three(group_norm_act(first_conv, norm2_gain, norm2_shift), conv2_weight)
    image_latent = conv_three(group_norm_act(hidden, head_gain, head_shift), head_weight) + head_bias
    frame_count = noisy_latents.shape[0]
    height = noisy_latents.shape[2]
    width = noisy_latents.shape[3]
    opening = jnp.arange(frame_count) == 0
    condition = jnp.where(opening[:, None, None, None], jnp.transpose(image_latent, (2, 0, 1))[None], later_cond)
    marks = jnp.broadcast_to(opening.astype(jnp.float32)[:, None, None, None], (frame_count, 4, height, width))
    stacked = jnp.concatenate([noisy_latents, marks, condition], axis=1)
    channel_count = stacked.shape[1]
    patches = stacked.reshape(frame_count, channel_count, height // 2, 2, width // 2, 2).transpose(0, 2, 4, 1, 3, 5).reshape(-1, channel_count * 4)
    tokens = jnp.dot(patches, patch_weight, precision=lax.Precision.HIGHEST, preferred_element_type=jnp.float32) + patch_bias
    return (tokens.reshape(frame_count, height // 2, width // 2, -1), image_latent)
```

```python
import functools

import jax
import jax.numpy as jnp
from jax import lax
from jax.experimental import pallas as pl
from jax.experimental.pallas import tpu as pltpu
from jax.sharding import PartitionSpec as P

NGROUP = 32


EPSILON = 1e-06
HIGHEST = lax.Precision.HIGHEST


def padded_2(cells, sides, width):
    for axis, dim in sides:
        count = lax.axis_size(axis)
        ends = count - 1
        head = lax.slice_in_dim(cells, 0, width, axis=dim)
        tail = lax.slice_in_dim(cells, cells.shape[dim] - width, cells.shape[dim], axis=dim)
        cells = jnp.concatenate(
            [
                lax.ppermute(tail, axis, [(i, (i + 1) % count) for i in range(ends)]),
                cells,
                lax.ppermute(head, axis, [((i + 1) % count, i) for i in range(ends)]),
            ],
            axis=dim,
        )
    return cells


def group_stats(inner, count_all):
    grouped = inner.reshape(-1, NGROUP, inner.shape[-1] // NGROUP)
    totals, squares = lax.psum(
        (jnp.sum(grouped, axis=(0, 2)), jnp.sum(grouped * grouped, axis=(0, 2))), ("space", "tm")
    )
    center = totals / count_all
    spread = squares / count_all - center * center
    return (center, lax.rsqrt(spread + EPSILON))


def normalize_act(values, stats, gain, shift):
    center, inverse = stats
    grouped = values.reshape(values.shape[:-1] + (NGROUP, values.shape[-1] // NGROUP))
    scaled = (grouped - center[:, None]) * inverse[:, None]
    return jax.nn.silu(scaled.reshape(values.shape) * gain + shift)


def tap_columns(padded, rows_out, cols_out):
    shifted = [
        padded[row_tap : row_tap + rows_out, col_tap : col_tap + cols_out, :]
        for row_tap in range(3)
        for col_tap in range(3)
    ]
    return jnp.stack(shifted, axis=2).reshape(rows_out * cols_out, 9, padded.shape[-1])


def add_taps(columns, piece):
    depth = piece.shape[2]
    picked = columns.reshape(columns.shape[0], 9 * depth)
    return jnp.dot(
        picked,
        piece.reshape(9 * depth, piece.shape[3]),
        precision=HIGHEST,
        preferred_element_type=jnp.float32,
    )


def wide_conv(padded, weight, rows_out, cols_out):
    columns = tap_columns(padded, rows_out, cols_out)
    summed = add_taps(columns, lax.all_gather(weight, "space", axis=2, tiled=True))
    return lax.all_gather(summed.reshape(rows_out, cols_out, -1), "chan", axis=2, tiled=True)


def border_rim(values):
    return padded_2(values, (("space", 0), ("tm", 1)), 1)


def on_device(
    features,
    norm1_gain,
    norm1_shift,
    conv1_weight,
    norm2_gain,
    norm2_shift,
    conv2_weight,
    head_gain,
    head_shift,
    head_weight,
    head_bias,
    noisy_latents,
    later_cond,
    patch_weight,
    patch_bias,
):
    tile_rows = features.shape[0]
    tile_cols = features.shape[1]
    count_all = float(
        tile_rows
        * tile_cols
        * lax.axis_size("space")
        * lax.axis_size("tm")
        * (features.shape[2] // NGROUP)
    )
    first_stats = group_stats(features, count_all)
    active = normalize_act(features, first_stats, norm1_gain, norm1_shift)
    first_conv = wide_conv(border_rim(active), conv1_weight, tile_rows, tile_cols)
    second_stats = group_stats(first_conv, count_all)
    second_act = normalize_act(first_conv, second_stats, norm2_gain, norm2_shift)
    second_conv = wide_conv(border_rim(second_act), conv2_weight, tile_rows, tile_cols)
    hidden = features + second_conv
    head_stats = group_stats(hidden, count_all)
    head_act = normalize_act(hidden, head_stats, head_gain, head_shift)
    head_pad = padded_2(head_act, (("space", 0), ("tm", 1)), 1)
    head_columns = tap_columns(head_pad, tile_rows, tile_cols)
    latent_part = (
        add_taps(head_columns, lax.all_gather(head_weight, "space", axis=2, tiled=True)) + head_bias
    )
    image_latent = lax.all_gather(
        latent_part.reshape(tile_rows, tile_cols, -1), "chan", axis=2, tiled=True
    )
    latent_row = lax.all_gather(image_latent, "tm", axis=1, tiled=True)
    frame_count = noisy_latents.shape[0]
    full_width = noisy_latents.shape[3]
    frame_ids = lax.axis_index("tm") * frame_count + jnp.arange(frame_count)
    opening = frame_ids == 0
    condition = jnp.where(
        opening[:, None, None, None], jnp.transpose(latent_row, (2, 0, 1))[None], later_cond
    )
    marks = jnp.broadcast_to(
        opening.astype(jnp.float32)[:, None, None, None], (frame_count, 4, tile_rows, full_width)
    )
    stacked = jnp.concatenate([noisy_latents, marks, condition], axis=1)
    channel_count = stacked.shape[1]
    patches = (
        stacked.reshape(frame_count, channel_count, tile_rows // 2, 2, full_width // 2, 2)
        .transpose(0, 2, 4, 1, 3, 5)
        .reshape(-1, channel_count * 4)
    )
    tokens = (
        jnp.dot(patches, patch_weight, precision=HIGHEST, preferred_element_type=jnp.float32)
        + patch_bias
    )
    return (tokens.reshape(frame_count, tile_rows // 2, full_width // 2, -1), image_latent)


MESH = pl.DeviceIdType.MESH
LANES = 128
BF16 = jnp.bfloat16
F32 = jnp.float32


def split_pair(values):
    high = values.astype(BF16)
    return high, (values - high.astype(F32)).astype(BF16)


def fused_kernel(
    dims,
    feat,
    gain1,
    shift1,
    w1_hbm,
    gain2,
    shift2,
    w2_hbm,
    gain3,
    shift3,
    head_w,
    head_b,
    noisy,
    later,
    pw_hbm,
    patch_b,
    tokens,
    latent,
    w1_raw,
    w2_raw,
    pw_raw,
    w1_mat,
    w2_mat,
    wh_mat,
    wn_mat,
    wc_mat,
    base,
    a_send,
    feat_all,
    conv_all,
    taps,
    msg,
    msg_in,
    piece,
    piece_in,
    lat_send,
    lat_in,
    cells,
    turned,
    patch,
    load_sem,
    a_ssem,
    a_rsem,
    m_ssem,
    m_rsem,
    sib_ssem,
    sib_rsem,
    p_ssem,
    p_rsem,
    l_ssem,
    l_rsem,
):
    S, T, C = dims["S"], dims["T"], dims["C"]
    R, W, CH = dims["R"], dims["W"], dims["CH"]
    Z, FR = dims["Z"], dims["FR"]
    CB = CH // S
    NH = CH // C
    BH = NH // CB
    H = S * R
    M = H * W
    HM = M // 2
    HR = H // 2
    TILE = R * W
    per_group = CH // NGROUP
    ZH = Z // C
    s = lax.axis_index("space")
    t = lax.axis_index("tm")
    c = lax.axis_index("chan")
    other = 1 - c

    loads = [
        pltpu.make_async_copy(src, dst, load_sem.at[k])
        for k, (src, dst) in enumerate(((w1_hbm, w1_raw), (w2_hbm, w2_raw)))
    ]
    strips = pw_raw.shape[0]
    loads += [
        pltpu.make_async_copy(
            pw_hbm.at[:, n * LANES : (n + 1) * LANES], pw_raw.at[n], load_sem.at[2 + n]
        )
        for n in range(strips)
    ]
    for load in loads:
        load.start()

    barrier = pltpu.get_barrier_semaphore()
    for ds in range(S):
        for dt in range(T):
            for dc in range(C):
                if ds or dt or dc:
                    pl.semaphore_signal(
                        barrier,
                        inc=1,
                        device_id={
                            "space": lax.rem(s + ds, S),
                            "tm": lax.rem(t + dt, T),
                            "chan": lax.rem(c + dc, C),
                        },
                        device_id_type=MESH,
                    )

    def padded(values, width):
        rows = values.shape[0]
        if width == values.shape[1]:
            return values
        return jnp.concatenate([values, jnp.zeros((rows, width - values.shape[1]), values.dtype)], axis=1)

    for r in range(R):
        line = feat[r]
        for j in range(S):
            a_send[j, r * W : (r + 1) * W, :] = padded(line[:, j * CB : (j + 1) * CB], LANES)

    pl.semaphore_wait(barrier, S * T * C - 1)

    def a_copy(step):
        peer = lax.rem(s + step, S)
        return pltpu.make_async_remote_copy(
            src_ref=a_send.at[peer],
            dst_ref=feat_all.at[pl.ds(pl.multiple_of(s * TILE, 8), TILE)],
            send_sem=a_ssem.at[peer],
            recv_sem=a_rsem.at[s],
            device_id={"space": peer},
            device_id_type=MESH,
        )

    def a_arrival(step):
        peer = lax.rem(s + step, S)
        return pltpu.make_async_remote_copy(
            src_ref=a_send.at[peer],
            dst_ref=feat_all.at[pl.ds(pl.multiple_of(peer * TILE, 8), TILE)],
            send_sem=a_ssem.at[peer],
            recv_sem=a_rsem.at[peer],
            device_id={"space": peer},
            device_id_type=MESH,
        )

    for step in range(1, S):
        a_copy(step).start()
    feat_all[pl.ds(pl.multiple_of(s * TILE, 8), TILE), :] = a_send[s]

    def pick_block(ref):
        row = ref[...]
        out = jnp.zeros((1, CB), F32)
        for j in range(S):
            out = jnp.where(s == j, row[:, j * CB : (j + 1) * CB], out)
        return padded(out, LANES)

    row_id = lax.broadcasted_iota(jnp.int32, (LANES, LANES), 0)
    col_id = lax.broadcasted_iota(jnp.int32, (LANES, LANES), 1)
    same = ((row_id // per_group) == (col_id // per_group)) & (row_id < CB) & (col_id < CB)
    member = jnp.where(same, 1.0, 0.0).astype(F32)

    def group_sum(row):
        wide = jnp.broadcast_to(row, (8, LANES))
        return jnp.dot(wide, member, precision=HIGHEST, preferred_element_type=F32)[0:1]

    def prepare(raw, mat):
        gap = jnp.zeros((LANES - CB, BH * LANES), BF16) if CB < LANES else None
        for tap in range(9):
            w = raw[tap]
            wide = jnp.concatenate(
                [padded(w[:, i * CB : (i + 1) * CB], LANES) for i in range(BH)], axis=1
            )
            high, low = split_pair(wide)
            store_split(mat, tap, high, low, gap)

    def store_split(mat, tap, high, low, gap):
        for place, value in ((2 * tap, high), (2 * tap + 1, high), (18 + tap, low)):
            mat[place * LANES : place * LANES + CB, :] = value
            if gap is not None:
                mat[place * LANES + CB : (place + 1) * LANES, :] = gap

    def channel_stats(values):
        total = jnp.sum(values, axis=0, keepdims=True)
        middle = total * (1.0 / HM)
        away = values - middle
        return total, jnp.sum(away * away, axis=0, keepdims=True)

    edge = HR
    pad_edge = dims["EDGE"]

    def exchange(k, full):
        start = pl.multiple_of(c * HM, 8)
        total, spread = channel_stats(full[pl.ds(start, HM), :])
        msg[k, 0:edge, :] = full[pl.ds(start, HR, stride=W), :]
        msg[k, pad_edge : pad_edge + edge, :] = full[pl.ds(start + (W - 1), HR, stride=W), :]
        msg[k, 2 * pad_edge : 2 * pad_edge + 1, :] = total
        msg[k, 2 * pad_edge + 1 : 2 * pad_edge + 2, :] = spread

        def copies(slot_t, slot_c, peer_t, peer_c, dc):
            return pltpu.make_async_remote_copy(
                src_ref=msg.at[k],
                dst_ref=msg_in.at[k, slot_t, slot_c],
                send_sem=m_ssem.at[k, peer_t, peer_c],
                recv_sem=m_rsem.at[k, slot_t, slot_c],
                device_id={"tm": peer_t, "chan": peer_c},
                device_id_type=MESH,
            )

        outgoing = []
        incoming = []
        for dt in range(1, T):
            for dc in range(C):
                peer_t = lax.rem(t + dt, T)
                peer_c = lax.rem(c + dc, C)
                outgoing.append(copies(t, c, peer_t, peer_c, dc))
                incoming.append(copies(peer_t, peer_c, peer_t, peer_c, dc))
        for copy in outgoing:
            copy.start()
        return outgoing, incoming

    def sibling(k, full, mine):
        start = pl.multiple_of(mine * HM, 8)
        return pltpu.make_async_remote_copy(
            src_ref=full.at[pl.ds(start, HM)],
            dst_ref=full.at[pl.ds(start, HM)],
            send_sem=sib_ssem.at[k],
            recv_sem=sib_rsem.at[k],
            device_id={"chan": other},
            device_id_type=MESH,
        )

    left = lax.rem(t + T - 1, T)
    right = lax.rem(t + 1, T)

    def activate(k, full, incoming, gain, shift):
        parts = [channel_stats(full[h * HM : (h + 1) * HM, :]) for h in range(2)]
        for copy in incoming:
            copy.wait_recv()
        for dt in range(1, T):
            peer_t = lax.rem(t + dt, T)
            for cc in range(C):
                parts.append(
                    (
                        msg_in[k, peer_t, cc, 2 * pad_edge : 2 * pad_edge + 1, :],
                        msg_in[k, peer_t, cc, 2 * pad_edge + 1 : 2 * pad_edge + 2, :],
                    )
                )
        scale = 1.0 / float(per_group * M * T)
        total = parts[0][0]
        for part in parts[1:]:
            total = total + part[0]
        center = group_sum(total) * scale
        gathered = jnp.zeros((1, LANES), F32)
        for part_total, part_spread in parts:
            away = part_total * (1.0 / HM) - center
            gathered = gathered + part_spread + away * away * float(HM)
        inverse = lax.rsqrt(group_sum(gathered) * scale + EPSILON)
        multiply = inverse

        def act(values):
            u = (values - center) * multiply * gain + shift
            return u / (1.0 + jnp.exp(-u))

        for h in range(2):
            value = act(full[h * HM : (h + 1) * HM, :])
            at = W + h * HM
            taps[1, at : at + HM, :] = value
            taps[0, at + 1 : at + 1 + HM, :] = value
            taps[2, at - 1 : at - 1 + HM, :] = value
        for h in range(C):
            from_left = act(msg_in[k, left, h, pad_edge : pad_edge + edge, :])
            from_right = act(msg_in[k, right, h, 0:edge, :])
            from_left = jnp.where(t > 0, from_left, 0.0)
            from_right = jnp.where(t < T - 1, from_right, 0.0)
            at = W + h * HM
            taps[0, pl.ds(at, HR, stride=W), :] = from_left
            taps[2, pl.ds(at + W - 1, HR, stride=W), :] = from_right
        zero = jnp.zeros((W, LANES), F32)
        tail = jnp.zeros((taps.shape[1] - W - M, LANES), F32)
        for b in range(3):
            taps[b, 0:W, :] = zero
            taps[b, W + M :, :] = tail

    def operand(start, rows):
        pairs = []
        for a in range(3):
            for b in range(3):
                pairs.append(split_pair(taps[b, start + a * W : start + a * W + rows, :]))
        return jnp.concatenate(
            [v for pair in pairs for v in pair] + [pair[0] for pair in pairs], axis=1
        )

    def piece_copy(k, i, h):
        block = c * BH + i
        return block, pltpu.make_async_remote_copy(
            src_ref=piece.at[k, i, h],
            dst_ref=piece_in.at[k, s],
            send_sem=p_ssem.at[k, i, h],
            recv_sem=p_rsem.at[k, s],
            device_id={"space": block, "chan": h},
            device_id_type=MESH,
        )

    def conv_send(k, mat):
        for h in range(2):
            part = jnp.dot(operand(h * HM, HM), mat[...], preferred_element_type=F32)
            for i in range(BH):
                piece[k, i, h] = part[:, i * LANES : (i + 1) * LANES]
                block, copy = piece_copy(k, i, h)
                away = jnp.logical_or(block != s, c != h)

                @pl.when(away)
                def _():
                    copy.start()

                @pl.when(jnp.logical_not(away))
                def _():
                    piece_in[k, s] = piece[k, i, h]

    def conv_receive(k, full, extra):
        holder = s // BH
        for step in range(S):
            source = lax.rem(s + step, S)
            arrival = pltpu.make_async_remote_copy(
                src_ref=piece.at[k, 0, 0],
                dst_ref=piece_in.at[k, source],
                send_sem=p_ssem.at[k, 0, 0],
                recv_sem=p_rsem.at[k, source],
                device_id={"space": source, "chan": holder},
                device_id_type=MESH,
            )
            if step == 0:

                @pl.when(holder != c)
                def _():
                    arrival.wait_recv()

            else:
                arrival.wait_recv()
        total = piece_in[k, 0]
        for j in range(1, S):
            total = total + piece_in[k, j]
        start = pl.multiple_of(c * HM, 8)
        if extra is not None:
            total = total + extra[pl.ds(start, HM), :]
        full[pl.ds(start, HM), :] = total

    def conv_drain(k):
        for h in range(2):
            for i in range(BH):
                block, copy = piece_copy(k, i, h)

                @pl.when(jnp.logical_or(block != s, c != h))
                def _():
                    copy.wait_send()

    loads[0].wait()
    prepare(w1_raw, w1_mat)
    for step in range(1, S):
        a_arrival(step).wait_recv()
    out1, in1 = exchange(0, feat_all)
    activate(0, feat_all, in1, pick_block(gain1), pick_block(shift1))
    conv_send(0, w1_mat)

    loads[1].wait()
    prepare(w2_raw, w2_mat)
    gap = jnp.zeros((LANES - CB, LANES), BF16) if CB < LANES else None
    for tap in range(9):
        high, low = split_pair(padded(head_w[tap], LANES))
        store_split(wh_mat, tap, high, low, gap)
    for load in loads[2:]:
        load.wait()
    for first, mat in ((0, wn_mat), (4 * (Z + 4), wc_mat)):
        for b in range(2):
            for a in range(2):
                at = (b * 2 + a) * Z
                for n in range(strips):
                    high, low = split_pair(pw_raw[n, pl.ds(first + a * 2 + b, Z, stride=4), :])
                    lanes = slice(n * LANES, (n + 1) * LANES)
                    mat[at : at + Z, lanes] = high
                    mat[4 * Z + at : 4 * Z + at + Z, lanes] = high
                    mat[8 * Z + at : 8 * Z + at + Z, lanes] = low
    mark_sum = jnp.concatenate(
        [
            jnp.sum(pw_raw[n, 4 * Z : 4 * (Z + 4), :], axis=0, keepdims=True)
            for n in range(strips)
        ],
        axis=1,
    )

    PR, PC, PP = dims["PR"], dims["PC"], dims["PP"]
    FULLW = W * T
    cells[...] = jnp.zeros(cells.shape, F32)
    patch[...] = jnp.zeros(patch.shape, F32)

    def patches_of_cells():
        turned[...] = cells[...].T
        for b in range(2):
            picked = turned[pl.ds(b, PC, stride=2), :]
            for p in range(PR):
                patch[p * PP : p * PP + PC, b * 2 * Z : (b + 1) * 2 * Z] = picked[
                    :, p * 2 * Z : (p + 1) * 2 * Z
                ]
        high, low = split_pair(patch[:, 0 : 4 * Z])
        return jnp.concatenate([high, low, high], axis=1)

    for f in range(FR):
        for i in range(R):
            cells[i * Z : (i + 1) * Z, 0:FULLW] = noisy[f, :, i, :]
        got = jnp.dot(patches_of_cells(), wn_mat[...], preferred_element_type=F32)
        opening = (t * FR + f) == 0
        base[f] = got + patch_b[...] + jnp.where(opening, mark_sum, 0.0)

    conv_receive(0, conv_all.at[0], None)
    sib1 = sibling(0, conv_all.at[0], c)
    sib1.start()
    out2, in2 = exchange(1, conv_all.at[0])
    sibling(0, conv_all.at[0], other).wait_recv()
    activate(1, conv_all.at[0], in2, pick_block(gain2), pick_block(shift2))
    conv_send(1, w2_mat)

    conv_receive(1, conv_all.at[1], feat_all)
    sib2 = sibling(1, conv_all.at[1], c)
    sib2.start()
    out3, in3 = exchange(2, conv_all.at[1])
    sibling(1, conv_all.at[1], other).wait_recv()
    activate(2, conv_all.at[1], in3, pick_block(gain3), pick_block(shift3))

    def lat_copy(dest_s, dest_t, dest_c, slot_s, slot_t, slot_c):
        return pltpu.make_async_remote_copy(
            src_ref=lat_send.at[dest_s],
            dst_ref=lat_in.at[slot_t, slot_c, slot_s],
            send_sem=l_ssem.at[dest_t, dest_c, dest_s],
            recv_sem=l_rsem.at[slot_t, slot_c, slot_s],
            device_id={"space": dest_s, "tm": dest_t, "chan": dest_c},
            device_id_type=MESH,
        )

    bias = jnp.where(s == 0, head_b[...], 0.0)
    for j in range(S):
        part = jnp.dot(operand(j * TILE, LANES), wh_mat[...], preferred_element_type=F32)
        lat_send[j] = part.T[0:ZH, :] + bias
    lat_in[t, c, s] = lat_send[s]
    lat_out = []
    lat_arrive = []
    for ds in reversed(range(S)):
        for dt in range(T):
            for dc in range(C):
                if ds or dt or dc:
                    ps = lax.rem(s + ds, S)
                    pt = lax.rem(t + dt, T)
                    pc = lax.rem(c + dc, C)
                    copy = lat_copy(ps, pt, pc, s, t, c)
                    copy.start()
                    lat_out.append(copy)
                    lat_arrive.append(lat_copy(ps, pt, pc, ps, pt, pc))

    conv_drain(0)
    conv_drain(1)
    for copy in out1 + out2 + out3 + [sib1, sib2]:
        copy.wait_send()
    for step in range(1, S):
        a_copy(step).wait_send()

    for copy in lat_arrive:
        copy.wait_recv()

    def half_latent(tt, cc):
        total = lat_in[tt, cc, 0]
        for j in range(1, S):
            total = total + lat_in[tt, cc, j]
        return total

    cells[...] = jnp.zeros(cells.shape, F32)
    for cc in range(C):
        cells[cc * ZH : (cc + 1) * ZH, :] = half_latent(t, cc)
    turned[...] = cells[...].T
    for r in range(R):
        latent[r] = turned[r * W : (r + 1) * W, 0:Z]
    for f in range(FR):
        cells[...] = jnp.zeros(cells.shape, F32)
        opening = (t * FR + f) == 0
        for tt in range(T):
            for cc in range(C):
                value = half_latent(tt, cc)
                for i in range(R):
                    at = i * Z + cc * ZH
                    cells[at : at + ZH, tt * W : (tt + 1) * W] = value[:, i * W : (i + 1) * W]
        for i in range(R):
            rows = slice(i * Z, (i + 1) * Z)
            cells[rows, 0:FULLW] = jnp.where(opening, cells[rows, 0:FULLW], later[f, :, i, :])
        got = base[f] + jnp.dot(patches_of_cells(), wc_mat[...], preferred_element_type=F32)
        for p in range(PR):
            tokens[f, p] = got[p * PP : p * PP + PC, :]
    for copy in lat_out:
        copy.wait_send()


def up(value, unit):
    return -(-value // unit) * unit


def plan(mesh_shape, features, noisy_latents, patch_weight):
    S, T, C = mesh_shape["space"], mesh_shape["tm"], mesh_shape["chan"]
    R, W, CH = features.shape
    FR, Z = noisy_latents.shape[:2]
    dims = dict(S=S, T=T, C=C, R=R, W=W, CH=CH, Z=Z, FR=FR)
    H = S * R
    dims["EDGE"] = up(H // 2, 8)
    dims["PR"], dims["PC"] = R // 2, W * T // 2
    dims["PP"] = up(W * T // 2, 8)
    dims["N"] = patch_weight.shape[1]
    fits = (
        C == 2
        and T > 1
        and S % C == 0
        and CH % S == 0
        and CH // S <= LANES
        and (CH // S) % (CH // NGROUP) == 0
        and (R * W) % 8 == 0
        and (H * W // 2) % 8 == 0
        and H % 2 == 0
        and R * W <= LANES
        and R * Z <= LANES
        and W * T <= LANES
        and 4 * Z <= LANES
        and dims["N"] % LANES == 0
        and H * W * LANES * 4 <= 2**19
    )
    return dims if fits else None


def fused(dims, args):
    S, T, C = dims["S"], dims["T"], dims["C"]
    R, W, CH = dims["R"], dims["W"], dims["CH"]
    Z, FR, N, EDGE = dims["Z"], dims["FR"], dims["N"], dims["EDGE"]
    CB, NH = CH // S, CH // C
    BH = NH // CB
    M = S * R * W
    MR = 2 * EDGE + 8
    (f, g1, s1, w1, g2, s2, w2, g3, s3, hw, hb, noisy, later, pw, pb) = args
    row = lambda v: v.reshape(1, v.shape[0])
    flat = lambda v: v.reshape((9,) + v.shape[2:])
    operands = (
        f, row(g1), row(s1), flat(w1), row(g2), row(s2), flat(w2), row(g3), row(s3),
        flat(hw), hb.reshape(-1, 1), noisy, later, pw, row(pb),
    )
    vmem = pl.BlockSpec(memory_space=pltpu.VMEM)
    far = pl.BlockSpec(memory_space=pl.ANY)
    in_specs = [far if k in (3, 6, 13) else vmem for k in range(15)]
    dma = pltpu.SemaphoreType.DMA
    big = lambda n: pltpu.VMEM((27 * LANES, n), BF16)
    scratch = [
        pltpu.VMEM((9, CB, NH), F32),
        pltpu.VMEM((9, CB, NH), F32),
        pltpu.VMEM((N // LANES, pw.shape[0], LANES), F32),
        big(BH * LANES),
        big(BH * LANES),
        big(LANES),
        pltpu.VMEM((12 * Z, N), BF16),
        pltpu.VMEM((12 * Z, N), BF16),
        pltpu.VMEM((FR, dims["PR"] * dims["PP"], N), F32),
        pltpu.VMEM((S, R * W, LANES), F32),
        pltpu.VMEM((M, LANES), F32),
        pltpu.VMEM((2, M, LANES), F32),
        pltpu.VMEM((3, up(M + 2 * W + LANES, 8), LANES), F32),
        pltpu.VMEM((3, MR, LANES), F32),
        pltpu.VMEM((3, T, C, MR, LANES), F32),
        pltpu.VMEM((2, BH, 2, M // 2, LANES), F32),
        pltpu.VMEM((2, S, M // 2, LANES), F32),
        pltpu.VMEM((S, Z // C, LANES), F32),
        pltpu.VMEM((T, C, S, Z // C, LANES), F32),
        pltpu.VMEM((LANES, LANES), F32),
        pltpu.VMEM((LANES, LANES), F32),
        pltpu.VMEM((dims["PR"] * dims["PP"], LANES), F32),
        dma((2 + N // LANES,)),
        dma((S,)),
        dma((S,)),
        dma((3, T, C)),
        dma((3, T, C)),
        dma((2,)),
        dma((2,)),
        dma((2, BH, 2)),
        dma((2, S)),
        dma((T, C, S)),
        dma((T, C, S)),
    ]
    return pl.pallas_call(
        functools.partial(fused_kernel, dims),
        out_shape=(
            jax.ShapeDtypeStruct((FR, dims["PR"], dims["PC"], N), F32),
            jax.ShapeDtypeStruct((R, W, Z), F32),
        ),
        in_specs=in_specs,
        out_specs=(vmem, vmem),
        scratch_shapes=scratch,
        compiler_params=pltpu.CompilerParams(
            collective_id=0, has_side_effects=True, vmem_limit_bytes=60 * 2**20
        ),
        name="fused_block",
    )(*operands)


def solution(mesh):
    shape = dict(mesh.shape)

    def step(*args):
        dims = plan(shape, args[0], args[11], args[13])
        return on_device(*args) if dims is None else fused(dims, args)

    return jax.shard_map(
        step,
        mesh=mesh,
        in_specs=(
            P(("groups", "space"), "tm", None),
            P(),
            P(),
            P(None, None, "space", "chan"),
            P(),
            P(),
            P(None, None, "space", "chan"),
            P(),
            P(),
            P(None, None, "space", "chan"),
            P("chan"),
            P(("groups", "tm"), None, "space", None),
            P(("groups", "tm"), None, "space", None),
            P(None, "chan"),
            P("chan"),
        ),
        out_specs=(P(("groups", "tm"), "space", None, "chan"), P(("groups", "space"), "tm", None)),
        check_vma=False,
    )
```

```python
import functools

import jax
import jax.numpy as jnp
from jax import lax
from jax.experimental import pallas as pl
from jax.experimental.pallas import tpu as pltpu
from jax.sharding import PartitionSpec as P

NGROUP = 32


EPSILON = 1e-06
HIGHEST = lax.Precision.HIGHEST


def padded_2(cells, sides, width):
    for axis, dim in sides:
        count = lax.axis_size(axis)
        ends = count - 1
        head = lax.slice_in_dim(cells, 0, width, axis=dim)
        tail = lax.slice_in_dim(cells, cells.shape[dim] - width, cells.shape[dim], axis=dim)
        cells = jnp.concatenate(
            [
                lax.ppermute(tail, axis, [(i, (i + 1) % count) for i in range(ends)]),
                cells,
                lax.ppermute(head, axis, [((i + 1) % count, i) for i in range(ends)]),
            ],
            axis=dim,
        )
    return cells


def group_stats(inner, count_all):
    grouped = inner.reshape(-1, NGROUP, inner.shape[-1] // NGROUP)
    totals, squares = lax.psum(
        (jnp.sum(grouped, axis=(0, 2)), jnp.sum(grouped * grouped, axis=(0, 2))), ("space", "tm")
    )
    center = totals / count_all
    spread = squares / count_all - center * center
    return (center, lax.rsqrt(spread + EPSILON))


def normalize_act(values, stats, gain, shift):
    center, inverse = stats
    grouped = values.reshape(values.shape[:-1] + (NGROUP, values.shape[-1] // NGROUP))
    scaled = (grouped - center[:, None]) * inverse[:, None]
    return jax.nn.silu(scaled.reshape(values.shape) * gain + shift)


def tap_columns(padded, rows_out, cols_out):
    shifted = [
        padded[row_tap : row_tap + rows_out, col_tap : col_tap + cols_out, :]
        for row_tap in range(3)
        for col_tap in range(3)
    ]
    return jnp.stack(shifted, axis=2).reshape(rows_out * cols_out, 9, padded.shape[-1])


def add_taps(columns, piece):
    depth = piece.shape[2]
    picked = columns.reshape(columns.shape[0], 9 * depth)
    return jnp.dot(
        picked,
        piece.reshape(9 * depth, piece.shape[3]),
        precision=HIGHEST,
        preferred_element_type=jnp.float32,
    )


def wide_conv(padded, weight, rows_out, cols_out):
    columns = tap_columns(padded, rows_out, cols_out)
    summed = add_taps(columns, lax.all_gather(weight, "space", axis=2, tiled=True))
    return lax.all_gather(summed.reshape(rows_out, cols_out, -1), "chan", axis=2, tiled=True)


def border_rim(values):
    return padded_2(values, (("space", 0), ("tm", 1)), 1)


def on_device(
    features,
    norm1_gain,
    norm1_shift,
    conv1_weight,
    norm2_gain,
    norm2_shift,
    conv2_weight,
    head_gain,
    head_shift,
    head_weight,
    head_bias,
    noisy_latents,
    later_cond,
    patch_weight,
    patch_bias,
):
    tile_rows = features.shape[0]
    tile_cols = features.shape[1]
    count_all = float(
        tile_rows
        * tile_cols
        * lax.axis_size("space")
        * lax.axis_size("tm")
        * (features.shape[2] // NGROUP)
    )
    first_stats = group_stats(features, count_all)
    active = normalize_act(features, first_stats, norm1_gain, norm1_shift)
    first_conv = wide_conv(border_rim(active), conv1_weight, tile_rows, tile_cols)
    second_stats = group_stats(first_conv, count_all)
    second_act = normalize_act(first_conv, second_stats, norm2_gain, norm2_shift)
    second_conv = wide_conv(border_rim(second_act), conv2_weight, tile_rows, tile_cols)
    hidden = features + second_conv
    head_stats = group_stats(hidden, count_all)
    head_act = normalize_act(hidden, head_stats, head_gain, head_shift)
    head_pad = padded_2(head_act, (("space", 0), ("tm", 1)), 1)
    head_columns = tap_columns(head_pad, tile_rows, tile_cols)
    latent_part = (
        add_taps(head_columns, lax.all_gather(head_weight, "space", axis=2, tiled=True)) + head_bias
    )
    image_latent = lax.all_gather(
        latent_part.reshape(tile_rows, tile_cols, -1), "chan", axis=2, tiled=True
    )
    latent_row = lax.all_gather(image_latent, "tm", axis=1, tiled=True)
    frame_count = noisy_latents.shape[0]
    full_width = noisy_latents.shape[3]
    frame_ids = lax.axis_index("tm") * frame_count + jnp.arange(frame_count)
    opening = frame_ids == 0
    condition = jnp.where(
        opening[:, None, None, None], jnp.transpose(latent_row, (2, 0, 1))[None], later_cond
    )
    marks = jnp.broadcast_to(
        opening.astype(jnp.float32)[:, None, None, None], (frame_count, 4, tile_rows, full_width)
    )
    stacked = jnp.concatenate([noisy_latents, marks, condition], axis=1)
    channel_count = stacked.shape[1]
    patches = (
        stacked.reshape(frame_count, channel_count, tile_rows // 2, 2, full_width // 2, 2)
        .transpose(0, 2, 4, 1, 3, 5)
        .reshape(-1, channel_count * 4)
    )
    tokens = (
        jnp.dot(patches, patch_weight, precision=HIGHEST, preferred_element_type=jnp.float32)
        + patch_bias
    )
    return (tokens.reshape(frame_count, tile_rows // 2, full_width // 2, -1), image_latent)


MESH = pl.DeviceIdType.MESH
LANES = 128
BF16 = jnp.bfloat16
F32 = jnp.float32


def split_pair(values):
    high = values.astype(BF16)
    return high, (values - high.astype(F32)).astype(BF16)


def fused_kernel(
    dims,
    feat_hbm,
    gain1_hbm,
    shift1_hbm,
    w1_hbm,
    gain2_hbm,
    shift2_hbm,
    w2_hbm,
    gain3_hbm,
    shift3_hbm,
    head_w_hbm,
    head_b_hbm,
    noisy_hbm,
    later_hbm,
    pw_hbm,
    patch_b_hbm,
    tokens,
    latent,
    feat,
    gain1,
    shift1,
    gain2,
    shift2,
    gain3,
    shift3,
    head_w,
    head_b,
    noisy,
    later,
    patch_b,
    w1_raw,
    w2_raw,
    pw_raw,
    w1_mat,
    w2_mat,
    wh_mat,
    wn_mat,
    wc_mat,
    base,
    a_send,
    feat_all,
    conv_all,
    taps,
    msg,
    msg_in,
    piece,
    piece_in,
    lat_send,
    lat_in,
    cells,
    turned,
    patch,
    load_sem,
    a_ssem,
    a_rsem,
    m_ssem,
    m_rsem,
    sib_ssem,
    sib_rsem,
    p_ssem,
    p_rsem,
    l_ssem,
    l_rsem,
):
    S, T, C = dims["S"], dims["T"], dims["C"]
    R, W, CH = dims["R"], dims["W"], dims["CH"]
    Z, FR = dims["Z"], dims["FR"]
    CB = CH // S
    NH = CH // C
    BH = NH // CB
    H = S * R
    M = H * W
    HM = M // 2
    HR = H // 2
    TILE = R * W
    per_group = CH // NGROUP
    ZH = Z // C
    s = lax.axis_index("space")
    t = lax.axis_index("tm")
    c = lax.axis_index("chan")
    other = 1 - c

    early = (
        (feat_hbm, feat), (w1_hbm, w1_raw), (gain1_hbm, gain1), (shift1_hbm, shift1),
        (w2_hbm, w2_raw), (gain2_hbm, gain2), (shift2_hbm, shift2),
        (gain3_hbm, gain3), (shift3_hbm, shift3), (head_w_hbm, head_w), (head_b_hbm, head_b),
        (noisy_hbm, noisy), (later_hbm, later), (patch_b_hbm, patch_b),
    )
    loads = [
        pltpu.make_async_copy(src, dst, load_sem.at[k]) for k, (src, dst) in enumerate(early)
    ]
    strips = pw_raw.shape[0]
    loads += [
        pltpu.make_async_copy(
            pw_hbm.at[:, n * LANES : (n + 1) * LANES], pw_raw.at[n], load_sem.at[len(early) + n]
        )
        for n in range(strips)
    ]
    for load in loads:
        load.start()

    barrier = pltpu.get_barrier_semaphore()
    for ds in range(S):
        for dt in range(T):
            for dc in range(C):
                if ds or dt or dc:
                    pl.semaphore_signal(
                        barrier,
                        inc=1,
                        device_id={
                            "space": lax.rem(s + ds, S),
                            "tm": lax.rem(t + dt, T),
                            "chan": lax.rem(c + dc, C),
                        },
                        device_id_type=MESH,
                    )

    def padded(values, width):
        rows = values.shape[0]
        if width == values.shape[1]:
            return values
        return jnp.concatenate([values, jnp.zeros((rows, width - values.shape[1]), values.dtype)], axis=1)

    loads[0].wait()
    for r in range(R):
        line = feat[r]
        for j in range(S):
            a_send[j, r * W : (r + 1) * W, :] = padded(line[:, j * CB : (j + 1) * CB], LANES)

    pl.semaphore_wait(barrier, S * T * C - 1)

    def a_copy(step):
        peer = lax.rem(s + step, S)
        return pltpu.make_async_remote_copy(
            src_ref=a_send.at[peer],
            dst_ref=feat_all.at[pl.ds(pl.multiple_of(s * TILE, 8), TILE)],
            send_sem=a_ssem.at[peer],
            recv_sem=a_rsem.at[s],
            device_id={"space": peer},
            device_id_type=MESH,
        )

    def a_arrival(step):
        peer = lax.rem(s + step, S)
        return pltpu.make_async_remote_copy(
            src_ref=a_send.at[peer],
            dst_ref=feat_all.at[pl.ds(pl.multiple_of(peer * TILE, 8), TILE)],
            send_sem=a_ssem.at[peer],
            recv_sem=a_rsem.at[peer],
            device_id={"space": peer},
            device_id_type=MESH,
        )

    for step in range(1, S):
        a_copy(step).start()
    feat_all[pl.ds(pl.multiple_of(s * TILE, 8), TILE), :] = a_send[s]

    def pick_block(ref):
        row = ref[...].reshape(1, CH)
        out = jnp.zeros((1, CB), F32)
        for j in range(S):
            out = jnp.where(s == j, row[:, j * CB : (j + 1) * CB], out)
        return padded(out, LANES)

    row_id = lax.broadcasted_iota(jnp.int32, (LANES, LANES), 0)
    col_id = lax.broadcasted_iota(jnp.int32, (LANES, LANES), 1)
    same = ((row_id // per_group) == (col_id // per_group)) & (row_id < CB) & (col_id < CB)
    member = jnp.where(same, 1.0, 0.0).astype(F32)

    def group_sum(row):
        wide = jnp.broadcast_to(row, (8, LANES))
        return jnp.dot(wide, member, precision=HIGHEST, preferred_element_type=F32)[0:1]

    def prepare(raw, mat):
        gap = jnp.zeros((LANES - CB, BH * LANES), BF16) if CB < LANES else None
        for tap in range(9):
            w = raw[tap]
            wide = jnp.concatenate(
                [padded(w[:, i * CB : (i + 1) * CB], LANES) for i in range(BH)], axis=1
            )
            high, low = split_pair(wide)
            store_split(mat, tap, high, low, gap)

    def store_split(mat, tap, high, low, gap):
        for place, value in ((2 * tap, high), (2 * tap + 1, high), (18 + tap, low)):
            mat[place * LANES : place * LANES + CB, :] = value
            if gap is not None:
                mat[place * LANES + CB : (place + 1) * LANES, :] = gap

    def channel_stats(values):
        total = jnp.sum(values, axis=0, keepdims=True)
        middle = total * (1.0 / HM)
        away = values - middle
        return total, jnp.sum(away * away, axis=0, keepdims=True)

    edge = HR
    pad_edge = dims["EDGE"]

    def exchange(k, full):
        start = pl.multiple_of(c * HM, 8)
        total, spread = channel_stats(full[pl.ds(start, HM), :])
        msg[k, 0:edge, :] = full[pl.ds(start, HR, stride=W), :]
        msg[k, pad_edge : pad_edge + edge, :] = full[pl.ds(start + (W - 1), HR, stride=W), :]
        msg[k, 2 * pad_edge : 2 * pad_edge + 1, :] = total
        msg[k, 2 * pad_edge + 1 : 2 * pad_edge + 2, :] = spread

        def copies(slot_t, slot_c, peer_t, peer_c, dc):
            return pltpu.make_async_remote_copy(
                src_ref=msg.at[k],
                dst_ref=msg_in.at[k, slot_t, slot_c],
                send_sem=m_ssem.at[k, peer_t, peer_c],
                recv_sem=m_rsem.at[k, slot_t, slot_c],
                device_id={"tm": peer_t, "chan": peer_c},
                device_id_type=MESH,
            )

        outgoing = []
        incoming = []
        for dt in range(1, T):
            for dc in range(C):
                peer_t = lax.rem(t + dt, T)
                peer_c = lax.rem(c + dc, C)
                outgoing.append(copies(t, c, peer_t, peer_c, dc))
                incoming.append(copies(peer_t, peer_c, peer_t, peer_c, dc))
        for copy in outgoing:
            copy.start()
        return outgoing, incoming

    def sibling(k, full, mine):
        start = pl.multiple_of(mine * HM, 8)
        return pltpu.make_async_remote_copy(
            src_ref=full.at[pl.ds(start, HM)],
            dst_ref=full.at[pl.ds(start, HM)],
            send_sem=sib_ssem.at[k],
            recv_sem=sib_rsem.at[k],
            device_id={"chan": other},
            device_id_type=MESH,
        )

    left = lax.rem(t + T - 1, T)
    right = lax.rem(t + 1, T)

    def activate(k, full, incoming, gain, shift):
        parts = [channel_stats(full[h * HM : (h + 1) * HM, :]) for h in range(2)]
        for copy in incoming:
            copy.wait_recv()
        for dt in range(1, T):
            peer_t = lax.rem(t + dt, T)
            for cc in range(C):
                parts.append(
                    (
                        msg_in[k, peer_t, cc, 2 * pad_edge : 2 * pad_edge + 1, :],
                        msg_in[k, peer_t, cc, 2 * pad_edge + 1 : 2 * pad_edge + 2, :],
                    )
                )
        scale = 1.0 / float(per_group * M * T)
        total = parts[0][0]
        for part in parts[1:]:
            total = total + part[0]
        center = group_sum(total) * scale
        gathered = jnp.zeros((1, LANES), F32)
        for part_total, part_spread in parts:
            away = part_total * (1.0 / HM) - center
            gathered = gathered + part_spread + away * away * float(HM)
        inverse = lax.rsqrt(group_sum(gathered) * scale + EPSILON)
        multiply = inverse

        def act(values):
            u = (values - center) * multiply * gain + shift
            return u / (1.0 + jnp.exp(-u))

        for h in range(2):
            value = act(full[h * HM : (h + 1) * HM, :])
            at = W + h * HM
            taps[1, at : at + HM, :] = value
            taps[0, at + 1 : at + 1 + HM, :] = value
            taps[2, at - 1 : at - 1 + HM, :] = value
        for h in range(C):
            from_left = act(msg_in[k, left, h, pad_edge : pad_edge + edge, :])
            from_right = act(msg_in[k, right, h, 0:edge, :])
            from_left = jnp.where(t > 0, from_left, 0.0)
            from_right = jnp.where(t < T - 1, from_right, 0.0)
            at = W + h * HM
            taps[0, pl.ds(at, HR, stride=W), :] = from_left
            taps[2, pl.ds(at + W - 1, HR, stride=W), :] = from_right
        zero = jnp.zeros((W, LANES), F32)
        tail = jnp.zeros((taps.shape[1] - W - M, LANES), F32)
        for b in range(3):
            taps[b, 0:W, :] = zero
            taps[b, W + M :, :] = tail

    def operand(start, rows):
        pairs = []
        for a in range(3):
            for b in range(3):
                pairs.append(split_pair(taps[b, start + a * W : start + a * W + rows, :]))
        return jnp.concatenate(
            [v for pair in pairs for v in pair] + [pair[0] for pair in pairs], axis=1
        )

    def piece_copy(k, i, h):
        block = c * BH + i
        return block, pltpu.make_async_remote_copy(
            src_ref=piece.at[k, i, h],
            dst_ref=piece_in.at[k, s],
            send_sem=p_ssem.at[k, i, h],
            recv_sem=p_rsem.at[k, s],
            device_id={"space": block, "chan": h},
            device_id_type=MESH,
        )

    def conv_send(k, mat):
        for h in range(2):
            part = jnp.dot(operand(h * HM, HM), mat[...], preferred_element_type=F32)
            for i in range(BH):
                piece[k, i, h] = part[:, i * LANES : (i + 1) * LANES]
                block, copy = piece_copy(k, i, h)
                away = jnp.logical_or(block != s, c != h)

                @pl.when(away)
                def _():
                    copy.start()

                @pl.when(jnp.logical_not(away))
                def _():
                    piece_in[k, s] = piece[k, i, h]

    def conv_receive(k, full, extra):
        holder = s // BH
        for step in range(S):
            source = lax.rem(s + step, S)
            arrival = pltpu.make_async_remote_copy(
                src_ref=piece.at[k, 0, 0],
                dst_ref=piece_in.at[k, source],
                send_sem=p_ssem.at[k, 0, 0],
                recv_sem=p_rsem.at[k, source],
                device_id={"space": source, "chan": holder},
                device_id_type=MESH,
            )
            if step == 0:

                @pl.when(holder != c)
                def _():
                    arrival.wait_recv()

            else:
                arrival.wait_recv()
        total = piece_in[k, 0]
        for j in range(1, S):
            total = total + piece_in[k, j]
        start = pl.multiple_of(c * HM, 8)
        if extra is not None:
            total = total + extra[pl.ds(start, HM), :]
        full[pl.ds(start, HM), :] = total

    def conv_drain(k):
        for h in range(2):
            for i in range(BH):
                block, copy = piece_copy(k, i, h)

                @pl.when(jnp.logical_or(block != s, c != h))
                def _():
                    copy.wait_send()

    for load in loads[1:4]:
        load.wait()
    prepare(w1_raw, w1_mat)
    for step in range(1, S):
        a_arrival(step).wait_recv()
    out1, in1 = exchange(0, feat_all)
    activate(0, feat_all, in1, pick_block(gain1), pick_block(shift1))
    conv_send(0, w1_mat)

    for load in loads[4:]:
        load.wait()
    prepare(w2_raw, w2_mat)
    for tap in range(9):
        high, low = split_pair(padded(head_w[tap], LANES))
        for place, value in ((2 * tap, high), (2 * tap + 1, high), (18 + tap, low)):
            wh_mat[:, place * LANES : (place + 1) * LANES] = value
    for first, mat in ((0, wn_mat), (4 * (Z + 4), wc_mat)):
        for b in range(2):
            for a in range(2):
                at = (b * 2 + a) * Z
                for n in range(strips):
                    high, low = split_pair(pw_raw[n, pl.ds(first + a * 2 + b, Z, stride=4), :])
                    lanes = slice(n * LANES, (n + 1) * LANES)
                    mat[at : at + Z, lanes] = high
                    mat[4 * Z + at : 4 * Z + at + Z, lanes] = high
                    mat[8 * Z + at : 8 * Z + at + Z, lanes] = low
    mark_sum = jnp.concatenate(
        [
            jnp.sum(pw_raw[n, 4 * Z : 4 * (Z + 4), :], axis=0, keepdims=True)
            for n in range(strips)
        ],
        axis=1,
    )

    PR, PC, PP = dims["PR"], dims["PC"], dims["PP"]
    FULLW = W * T
    cells[...] = jnp.zeros(cells.shape, F32)
    patch[...] = jnp.zeros(patch.shape, F32)

    def patches_of_cells():
        turned[...] = cells[...].T
        for b in range(2):
            picked = turned[pl.ds(b, PC, stride=2), :]
            for p in range(PR):
                patch[p * PP : p * PP + PC, b * 2 * Z : (b + 1) * 2 * Z] = picked[
                    :, p * 2 * Z : (p + 1) * 2 * Z
                ]
        high, low = split_pair(patch[:, 0 : 4 * Z])
        return jnp.concatenate([high, low, high], axis=1)

    for f in range(FR):
        for i in range(R):
            cells[i * Z : (i + 1) * Z, 0:FULLW] = noisy[f, i]
        got = jnp.dot(patches_of_cells(), wn_mat[...], preferred_element_type=F32)
        opening = (t * FR + f) == 0
        base[f] = got + patch_b[...].reshape(1, -1) + jnp.where(opening, mark_sum, 0.0)

    conv_receive(0, conv_all.at[0], None)
    sib1 = sibling(0, conv_all.at[0], c)
    sib1.start()
    out2, in2 = exchange(1, conv_all.at[0])
    sibling(0, conv_all.at[0], other).wait_recv()
    activate(1, conv_all.at[0], in2, pick_block(gain2), pick_block(shift2))
    conv_send(1, w2_mat)

    conv_receive(1, conv_all.at[1], feat_all)
    sib2 = sibling(1, conv_all.at[1], c)
    sib2.start()
    out3, in3 = exchange(2, conv_all.at[1])
    sibling(1, conv_all.at[1], other).wait_recv()
    activate(2, conv_all.at[1], in3, pick_block(gain3), pick_block(shift3))

    def lat_copy(dest_s, dest_t, dest_c, slot_s, slot_t, slot_c):
        return pltpu.make_async_remote_copy(
            src_ref=lat_send.at[dest_s],
            dst_ref=lat_in.at[slot_t, slot_c, slot_s],
            send_sem=l_ssem.at[dest_t, dest_c, dest_s],
            recv_sem=l_rsem.at[slot_t, slot_c, slot_s],
            device_id={"space": dest_s, "tm": dest_t, "chan": dest_c},
            device_id_type=MESH,
        )

    bias_row = jnp.broadcast_to(head_b[...].reshape(1, ZH), (ZH, ZH))
    diagonal = lax.broadcasted_iota(jnp.int32, (ZH, ZH), 0) == lax.broadcasted_iota(
        jnp.int32, (ZH, ZH), 1
    )
    bias = jnp.sum(jnp.where(diagonal & (s == 0), bias_row, 0.0), axis=1, keepdims=True)
    for j in range(S):
        part = lax.dot_general(
            wh_mat[...],
            operand(j * TILE, LANES),
            (((1,), (1,)), ((), ())),
            preferred_element_type=F32,
        )
        lat_send[j] = part + bias
    lat_in[t, c, s] = lat_send[s]
    lat_out = []
    lat_arrive = []
    for ds in reversed(range(S)):
        for dt in range(T):
            for dc in range(C):
                if ds or dt or dc:
                    ps = lax.rem(s + ds, S)
                    pt = lax.rem(t + dt, T)
                    pc = lax.rem(c + dc, C)
                    copy = lat_copy(ps, pt, pc, s, t, c)
                    copy.start()
                    lat_out.append(copy)
                    lat_arrive.append(lat_copy(ps, pt, pc, ps, pt, pc))

    conv_drain(0)
    conv_drain(1)
    for copy in out1 + out2 + out3 + [sib1, sib2]:
        copy.wait_send()
    for step in range(1, S):
        a_copy(step).wait_send()

    for copy in lat_arrive:
        copy.wait_recv()

    def half_latent(tt, cc):
        total = lat_in[tt, cc, 0]
        for j in range(1, S):
            total = total + lat_in[tt, cc, j]
        return total

    for cc in range(C):
        value = half_latent(t, cc)
        for r in range(R):
            latent[r, cc * ZH : (cc + 1) * ZH, :] = value[:, r * W : (r + 1) * W]
    for f in range(FR):
        cells[...] = jnp.zeros(cells.shape, F32)
        opening = (t * FR + f) == 0
        for tt in range(T):
            for cc in range(C):
                value = half_latent(tt, cc)
                for i in range(R):
                    at = i * Z + cc * ZH
                    cells[at : at + ZH, tt * W : (tt + 1) * W] = value[:, i * W : (i + 1) * W]
        for i in range(R):
            rows = slice(i * Z, (i + 1) * Z)
            cells[rows, 0:FULLW] = jnp.where(opening, cells[rows, 0:FULLW], later[f, i])
        got = base[f] + jnp.dot(patches_of_cells(), wc_mat[...], preferred_element_type=F32)
        for p in range(PR):
            tokens[p, :, f, :] = got[p * PP : p * PP + PC, :]
    for copy in lat_out:
        copy.wait_send()


def up(value, unit):
    return -(-value // unit) * unit


def plan(mesh_shape, features, noisy_latents, patch_weight):
    S, T, C = mesh_shape["space"], mesh_shape["tm"], mesh_shape["chan"]
    R, W, CH = features.shape
    FR, Z = noisy_latents.shape[:2]
    dims = dict(S=S, T=T, C=C, R=R, W=W, CH=CH, Z=Z, FR=FR)
    H = S * R
    dims["EDGE"] = up(H // 2, 8)
    dims["PR"], dims["PC"] = R // 2, W * T // 2
    dims["PP"] = up(W * T // 2, 8)
    dims["N"] = patch_weight.shape[1]
    fits = (
        C == 2
        and T > 1
        and S % C == 0
        and CH % S == 0
        and CH // S <= LANES
        and (CH // S) % (CH // NGROUP) == 0
        and (R * W) % 8 == 0
        and (H * W // 2) % 8 == 0
        and H % 2 == 0
        and R * W <= LANES
        and R * Z <= LANES
        and W * T <= LANES
        and 4 * Z <= LANES
        and dims["N"] % LANES == 0
        and H * W * LANES * 4 <= 2**19
    )
    return dims if fits else None


def fused(dims, args):
    S, T, C = dims["S"], dims["T"], dims["C"]
    R, W, CH = dims["R"], dims["W"], dims["CH"]
    Z, FR, N, EDGE = dims["Z"], dims["FR"], dims["N"], dims["EDGE"]
    CB, NH = CH // S, CH // C
    BH = NH // CB
    M = S * R * W
    MR = 2 * EDGE + 8
    (f, g1, s1, w1, g2, s2, w2, g3, s3, hw, hb, noisy, later, pw, pb) = args
    flat = lambda v: v.reshape((9,) + v.shape[2:])
    by_row = lambda v: jnp.transpose(v, (0, 2, 1, 3))
    operands = (
        f, g1, s1, flat(w1), g2, s2, flat(w2), g3, s3,
        flat(jnp.transpose(hw, (0, 1, 3, 2))), hb, by_row(noisy), by_row(later), pw, pb,
    )
    vmem = pl.BlockSpec(memory_space=pltpu.VMEM)
    in_specs = [pl.BlockSpec(memory_space=pl.ANY)] * 15
    dma = pltpu.SemaphoreType.DMA
    big = lambda n: pltpu.VMEM((27 * LANES, n), BF16)
    scratch = [
        pltpu.VMEM(operands[k].shape, F32) for k in (0, 1, 2, 4, 5, 7, 8, 9, 10, 11, 12, 14)
    ] + [
        pltpu.VMEM((9, CB, NH), F32),
        pltpu.VMEM((9, CB, NH), F32),
        pltpu.VMEM((N // LANES, pw.shape[0], LANES), F32),
        big(BH * LANES),
        big(BH * LANES),
        pltpu.VMEM((Z // C, 27 * LANES), BF16),
        pltpu.VMEM((12 * Z, N), BF16),
        pltpu.VMEM((12 * Z, N), BF16),
        pltpu.VMEM((FR, dims["PR"] * dims["PP"], N), F32),
        pltpu.VMEM((S, R * W, LANES), F32),
        pltpu.VMEM((M, LANES), F32),
        pltpu.VMEM((2, M, LANES), F32),
        pltpu.VMEM((3, up(M + 2 * W + LANES, 8), LANES), F32),
        pltpu.VMEM((3, MR, LANES), F32),
        pltpu.VMEM((3, T, C, MR, LANES), F32),
        pltpu.VMEM((2, BH, 2, M // 2, LANES), F32),
        pltpu.VMEM((2, S, M // 2, LANES), F32),
        pltpu.VMEM((S, Z // C, LANES), F32),
        pltpu.VMEM((T, C, S, Z // C, LANES), F32),
        pltpu.VMEM((LANES, LANES), F32),
        pltpu.VMEM((LANES, LANES), F32),
        pltpu.VMEM((dims["PR"] * dims["PP"], LANES), F32),
        dma((14 + N // LANES,)),
        dma((S,)),
        dma((S,)),
        dma((3, T, C)),
        dma((3, T, C)),
        dma((2,)),
        dma((2,)),
        dma((2, BH, 2)),
        dma((2, S)),
        dma((T, C, S)),
        dma((T, C, S)),
    ]
    tokens, latent = pl.pallas_call(
        functools.partial(fused_kernel, dims),
        out_shape=(
            jax.ShapeDtypeStruct((dims["PR"], dims["PC"], FR, N), F32),
            jax.ShapeDtypeStruct((R, Z, W), F32),
        ),
        in_specs=in_specs,
        out_specs=(vmem, vmem),
        scratch_shapes=scratch,
        compiler_params=pltpu.CompilerParams(
            collective_id=0, has_side_effects=True, vmem_limit_bytes=60 * 2**20
        ),
        name="fused_block",
    )(*operands)
    return jnp.transpose(tokens, (2, 0, 1, 3)), jnp.transpose(latent, (0, 2, 1))


def solution(mesh):
    shape = dict(mesh.shape)

    def step(*args):
        dims = plan(shape, args[0], args[11], args[13])
        return on_device(*args) if dims is None else fused(dims, args)

    return jax.shard_map(
        step,
        mesh=mesh,
        in_specs=(
            P(("groups", "space"), "tm", None),
            P(),
            P(),
            P(None, None, "space", "chan"),
            P(),
            P(),
            P(None, None, "space", "chan"),
            P(),
            P(),
            P(None, None, "space", "chan"),
            P("chan"),
            P(("groups", "tm"), None, "space", None),
            P(("groups", "tm"), None, "space", None),
            P(None, "chan"),
            P("chan"),
        ),
        out_specs=(P(("groups", "tm"), "space", None, "chan"), P(("groups", "space"), "tm", None)),
        check_vma=False,
    )
```

```python
import functools

import jax
import jax.numpy as jnp
from jax import lax
from jax.experimental import pallas as pl
from jax.experimental.pallas import tpu as pltpu
from jax.sharding import PartitionSpec as P

NGROUP = 32


EPSILON = 1e-06
HIGHEST = lax.Precision.HIGHEST


def padded_2(cells, sides, width):
    for axis, dim in sides:
        count = lax.axis_size(axis)
        ends = count - 1
        head = lax.slice_in_dim(cells, 0, width, axis=dim)
        tail = lax.slice_in_dim(cells, cells.shape[dim] - width, cells.shape[dim], axis=dim)
        cells = jnp.concatenate(
            [
                lax.ppermute(tail, axis, [(i, (i + 1) % count) for i in range(ends)]),
                cells,
                lax.ppermute(head, axis, [((i + 1) % count, i) for i in range(ends)]),
            ],
            axis=dim,
        )
    return cells


def group_stats(inner, count_all):
    grouped = inner.reshape(-1, NGROUP, inner.shape[-1] // NGROUP)
    totals, squares = lax.psum(
        (jnp.sum(grouped, axis=(0, 2)), jnp.sum(grouped * grouped, axis=(0, 2))), ("space", "tm")
    )
    center = totals / count_all
    spread = squares / count_all - center * center
    return (center, lax.rsqrt(spread + EPSILON))


def normalize_act(values, stats, gain, shift):
    center, inverse = stats
    grouped = values.reshape(values.shape[:-1] + (NGROUP, values.shape[-1] // NGROUP))
    scaled = (grouped - center[:, None]) * inverse[:, None]
    return jax.nn.silu(scaled.reshape(values.shape) * gain + shift)


def tap_columns(padded, rows_out, cols_out):
    shifted = [
        padded[row_tap : row_tap + rows_out, col_tap : col_tap + cols_out, :]
        for row_tap in range(3)
        for col_tap in range(3)
    ]
    return jnp.stack(shifted, axis=2).reshape(rows_out * cols_out, 9, padded.shape[-1])


def add_taps(columns, piece):
    depth = piece.shape[2]
    picked = columns.reshape(columns.shape[0], 9 * depth)
    return jnp.dot(
        picked,
        piece.reshape(9 * depth, piece.shape[3]),
        precision=HIGHEST,
        preferred_element_type=jnp.float32,
    )


def wide_conv(padded, weight, rows_out, cols_out):
    columns = tap_columns(padded, rows_out, cols_out)
    summed = add_taps(columns, lax.all_gather(weight, "space", axis=2, tiled=True))
    return lax.all_gather(summed.reshape(rows_out, cols_out, -1), "chan", axis=2, tiled=True)


def border_rim(values):
    return padded_2(values, (("space", 0), ("tm", 1)), 1)


def on_device(
    features,
    norm1_gain,
    norm1_shift,
    conv1_weight,
    norm2_gain,
    norm2_shift,
    conv2_weight,
    head_gain,
    head_shift,
    head_weight,
    head_bias,
    noisy_latents,
    later_cond,
    patch_weight,
    patch_bias,
):
    tile_rows = features.shape[0]
    tile_cols = features.shape[1]
    count_all = float(
        tile_rows
        * tile_cols
        * lax.axis_size("space")
        * lax.axis_size("tm")
        * (features.shape[2] // NGROUP)
    )
    first_stats = group_stats(features, count_all)
    active = normalize_act(features, first_stats, norm1_gain, norm1_shift)
    first_conv = wide_conv(border_rim(active), conv1_weight, tile_rows, tile_cols)
    second_stats = group_stats(first_conv, count_all)
    second_act = normalize_act(first_conv, second_stats, norm2_gain, norm2_shift)
    second_conv = wide_conv(border_rim(second_act), conv2_weight, tile_rows, tile_cols)
    hidden = features + second_conv
    head_stats = group_stats(hidden, count_all)
    head_act = normalize_act(hidden, head_stats, head_gain, head_shift)
    head_pad = padded_2(head_act, (("space", 0), ("tm", 1)), 1)
    head_columns = tap_columns(head_pad, tile_rows, tile_cols)
    latent_part = (
        add_taps(head_columns, lax.all_gather(head_weight, "space", axis=2, tiled=True)) + head_bias
    )
    image_latent = lax.all_gather(
        latent_part.reshape(tile_rows, tile_cols, -1), "chan", axis=2, tiled=True
    )
    latent_row = lax.all_gather(image_latent, "tm", axis=1, tiled=True)
    frame_count = noisy_latents.shape[0]
    full_width = noisy_latents.shape[3]
    frame_ids = lax.axis_index("tm") * frame_count + jnp.arange(frame_count)
    opening = frame_ids == 0
    condition = jnp.where(
        opening[:, None, None, None], jnp.transpose(latent_row, (2, 0, 1))[None], later_cond
    )
    marks = jnp.broadcast_to(
        opening.astype(jnp.float32)[:, None, None, None], (frame_count, 4, tile_rows, full_width)
    )
    stacked = jnp.concatenate([noisy_latents, marks, condition], axis=1)
    channel_count = stacked.shape[1]
    patches = (
        stacked.reshape(frame_count, channel_count, tile_rows // 2, 2, full_width // 2, 2)
        .transpose(0, 2, 4, 1, 3, 5)
        .reshape(-1, channel_count * 4)
    )
    tokens = (
        jnp.dot(patches, patch_weight, precision=HIGHEST, preferred_element_type=jnp.float32)
        + patch_bias
    )
    return (tokens.reshape(frame_count, tile_rows // 2, full_width // 2, -1), image_latent)


MESH = pl.DeviceIdType.MESH
LANES = 128
BF16 = jnp.bfloat16
F32 = jnp.float32


def split_pair(values):
    high = values.astype(BF16)
    return high, (values - high.astype(F32)).astype(BF16)


def fused_kernel(
    dims,
    feat_hbm,
    gain1_hbm,
    shift1_hbm,
    w1_hbm,
    gain2_hbm,
    shift2_hbm,
    w2_hbm,
    gain3_hbm,
    shift3_hbm,
    head_w_hbm,
    head_b_hbm,
    noisy_hbm,
    later_hbm,
    pw_hbm,
    patch_b_hbm,
    tokens,
    latent,
    feat,
    gain1,
    shift1,
    gain2,
    shift2,
    gain3,
    shift3,
    head_w,
    head_b,
    noisy,
    later,
    patch_b,
    w1_raw,
    w2_raw,
    pw_raw,
    w1_mat,
    w2_mat,
    wh_mat,
    wn_mat,
    wc_mat,
    base,
    a_send,
    a_pack,
    a_in,
    rim,
    rim_in,
    feat_all,
    conv_all,
    taps,
    msg,
    msg_in,
    piece,
    piece_in,
    lat_send,
    lat_in,
    cells,
    turned,
    patch,
    load_sem,
    a_ssem,
    a_rsem,
    f_ssem,
    f_rsem,
    r_ssem,
    r_rsem,
    m_ssem,
    m_rsem,
    sib_ssem,
    sib_rsem,
    p_ssem,
    p_rsem,
    l_ssem,
    l_rsem,
):
    S, T, C = dims["S"], dims["T"], dims["C"]
    R, W, CH = dims["R"], dims["W"], dims["CH"]
    Z, FR = dims["Z"], dims["FR"]
    CB = CH // S
    NH = CH // C
    BH = NH // CB
    H = S * R
    M = H * W
    HM = M // 2
    HR = H // 2
    TILE = R * W
    per_group = CH // NGROUP
    ZH = Z // C
    s = lax.axis_index("space")
    t = lax.axis_index("tm")
    c = lax.axis_index("chan")
    other = 1 - c

    early = (
        (feat_hbm, feat), (w1_hbm, w1_raw), (gain1_hbm, gain1), (shift1_hbm, shift1),
        (w2_hbm, w2_raw), (gain2_hbm, gain2), (shift2_hbm, shift2),
        (gain3_hbm, gain3), (shift3_hbm, shift3), (head_w_hbm, head_w), (head_b_hbm, head_b),
        (noisy_hbm, noisy), (later_hbm, later), (patch_b_hbm, patch_b),
    )
    loads = [
        pltpu.make_async_copy(src, dst, load_sem.at[k]) for k, (src, dst) in enumerate(early)
    ]
    strips = pw_raw.shape[0]
    loads += [
        pltpu.make_async_copy(
            pw_hbm.at[:, n * LANES : (n + 1) * LANES], pw_raw.at[n], load_sem.at[len(early) + n]
        )
        for n in range(strips)
    ]
    for load in loads:
        load.start()

    barrier = pltpu.get_barrier_semaphore()
    for ds in range(S):
        for dt in range(T):
            for dc in range(C):
                if ds or dt or dc:
                    pl.semaphore_signal(
                        barrier,
                        inc=1,
                        device_id={
                            "space": lax.rem(s + ds, S),
                            "tm": lax.rem(t + dt, T),
                            "chan": lax.rem(c + dc, C),
                        },
                        device_id_type=MESH,
                    )

    def padded(values, width):
        rows = values.shape[0]
        if width == values.shape[1]:
            return values
        return jnp.concatenate([values, jnp.zeros((rows, width - values.shape[1]), values.dtype)], axis=1)

    loads[0].wait()
    for r in range(R):
        line = feat[r]
        for j in range(S):
            a_send[j, r * W : (r + 1) * W, :] = padded(line[:, j * CB : (j + 1) * CB], LANES)

    def pack(dst, value, main):
        rows = value.shape[0]
        dst[...] = value[0:main]
        rest = rows - main
        free = LANES - CB
        for j in range(CB // free if rest else 0):
            dst[j * rest : (j + 1) * rest, CB:LANES] = value[main:rows, j * free : (j + 1) * free]

    def unpack(value, rows):
        main = value.shape[0]
        rest = rows - main
        if not rest:
            return (value,)
        free = LANES - CB
        columns = [value[j * rest : (j + 1) * rest, CB:LANES] for j in range(CB // free)]
        return value, padded(jnp.concatenate(columns, axis=1), LANES)

    def channel_stats(values):
        total = jnp.sum(values, axis=0, keepdims=True)
        middle = total * (1.0 / values.shape[0])
        away = values - middle
        return total, jnp.sum(away * away, axis=0, keepdims=True)

    AM, PM, RE = dims["AM"], dims["PM"], dims["RE"]
    AH = AM // 2
    for j in range(S):
        pack(a_pack.at[j], a_send[j], AM)

    pl.semaphore_wait(barrier, S * T * C - 1)

    def a_copy(step, sent):
        peer = lax.rem(s + step, S)
        slot = s if sent else peer
        mine = pl.ds(pl.multiple_of(c * AH, 8), AH)
        return pltpu.make_async_remote_copy(
            src_ref=a_pack.at[peer, mine],
            dst_ref=a_in.at[slot, mine],
            send_sem=a_ssem.at[peer],
            recv_sem=a_rsem.at[slot],
            device_id={"space": peer},
            device_id_type=MESH,
        )

    def a_forward(step, half):
        source = lax.rem(s + step, S)
        rows = pl.ds(pl.multiple_of(half * AH, 8), AH)
        return pltpu.make_async_remote_copy(
            src_ref=a_in.at[source, rows],
            dst_ref=a_in.at[source, rows],
            send_sem=f_ssem.at[source],
            recv_sem=f_rsem.at[source],
            device_id={"chan": other},
            device_id_type=MESH,
        )

    def rim_copy(dt, j, sent):
        peer = lax.rem(t + dt, T)
        slot_t, slot_s = (t, s) if sent else (peer, j)
        return pltpu.make_async_remote_copy(
            src_ref=rim.at[j],
            dst_ref=rim_in.at[slot_t, slot_s],
            send_sem=r_ssem.at[peer, j],
            recv_sem=r_rsem.at[slot_t, slot_s],
            device_id={"space": j, "tm": peer},
            device_id_type=MESH,
        )

    for step in range(1, S):
        a_copy(step, True).start()
    for j in range(S):
        total, spread = channel_stats(a_send[j])
        rim[j, 0:R, :] = a_send[j, pl.ds(0, R, stride=W), :]
        rim[j, RE : RE + R, :] = a_send[j, pl.ds(W - 1, R, stride=W), :]
        rim[j, 2 * RE : 2 * RE + 1, :] = total
        rim[j, 2 * RE + 1 : 2 * RE + 2, :] = spread
    for dt in range(1, T):
        for j in range(S):
            rim_copy(dt, j, True).start()
    feat_all[pl.ds(pl.multiple_of(s * TILE, 8), TILE), :] = a_send[s]

    def pick_block(ref):
        row = ref[...].reshape(1, CH)
        out = jnp.zeros((1, CB), F32)
        for j in range(S):
            out = jnp.where(s == j, row[:, j * CB : (j + 1) * CB], out)
        return padded(out, LANES)

    row_id = lax.broadcasted_iota(jnp.int32, (LANES, LANES), 0)
    col_id = lax.broadcasted_iota(jnp.int32, (LANES, LANES), 1)
    same = ((row_id // per_group) == (col_id // per_group)) & (row_id < CB) & (col_id < CB)
    member = jnp.where(same, 1.0, 0.0).astype(F32)

    def group_sum(row):
        wide = jnp.broadcast_to(row, (8, LANES))
        return jnp.dot(wide, member, precision=HIGHEST, preferred_element_type=F32)[0:1]

    def prepare(raw, mat):
        gap = jnp.zeros((LANES - CB, BH * LANES), BF16) if CB < LANES else None
        for tap in range(9):
            w = raw[tap]
            wide = jnp.concatenate(
                [padded(w[:, i * CB : (i + 1) * CB], LANES) for i in range(BH)], axis=1
            )
            high, low = split_pair(wide)
            store_split(mat, tap, high, low, gap)

    def store_split(mat, tap, high, low, gap):
        for place, value in ((2 * tap, high), (2 * tap + 1, high), (18 + tap, low)):
            mat[place * LANES : place * LANES + CB, :] = value
            if gap is not None:
                mat[place * LANES + CB : (place + 1) * LANES, :] = gap

    edge = HR
    pad_edge = dims["EDGE"]

    def exchange(k, full):
        start = pl.multiple_of(c * HM, 8)
        total, spread = channel_stats(full[pl.ds(start, HM), :])
        msg[k, 0:edge, :] = full[pl.ds(start, HR, stride=W), :]
        msg[k, pad_edge : pad_edge + edge, :] = full[pl.ds(start + (W - 1), HR, stride=W), :]
        msg[k, 2 * pad_edge : 2 * pad_edge + 1, :] = total
        msg[k, 2 * pad_edge + 1 : 2 * pad_edge + 2, :] = spread

        def copies(slot_t, slot_c, peer_t, peer_c, dc):
            return pltpu.make_async_remote_copy(
                src_ref=msg.at[k],
                dst_ref=msg_in.at[k, slot_t, slot_c],
                send_sem=m_ssem.at[k, peer_t, peer_c],
                recv_sem=m_rsem.at[k, slot_t, slot_c],
                device_id={"tm": peer_t, "chan": peer_c},
                device_id_type=MESH,
            )

        outgoing = []
        incoming = []
        for dt in range(1, T):
            for dc in range(C):
                peer_t = lax.rem(t + dt, T)
                peer_c = lax.rem(c + dc, C)
                outgoing.append(copies(t, c, peer_t, peer_c, dc))
                incoming.append(copies(peer_t, peer_c, peer_t, peer_c, dc))
        for copy in outgoing:
            copy.start()
        return outgoing, incoming

    def sibling(k, full, mine):
        start = pl.multiple_of(mine * HM, 8)
        return pltpu.make_async_remote_copy(
            src_ref=full.at[pl.ds(start, HM)],
            dst_ref=full.at[pl.ds(start, HM)],
            send_sem=sib_ssem.at[k],
            recv_sem=sib_rsem.at[k],
            device_id={"chan": other},
            device_id_type=MESH,
        )

    left = lax.rem(t + T - 1, T)
    right = lax.rem(t + 1, T)

    def activate(full, remote, rims, gain, shift):
        parts = [channel_stats(full[h * HM : (h + 1) * HM, :]) + (HM,) for h in range(2)]
        parts += remote
        scale = 1.0 / float(per_group * M * T)
        total = parts[0][0]
        for part in parts[1:]:
            total = total + part[0]
        center = group_sum(total) * scale
        gathered = jnp.zeros((1, LANES), F32)
        for part_total, part_spread, count in parts:
            away = part_total * (1.0 / count) - center
            gathered = gathered + part_spread + away * away * float(count)
        inverse = lax.rsqrt(group_sum(gathered) * scale + EPSILON)
        multiply = inverse

        def act(values):
            u = (values - center) * multiply * gain + shift
            return u / (1.0 + jnp.exp(-u))

        for h in range(2):
            value = act(full[h * HM : (h + 1) * HM, :])
            at = W + h * HM
            taps[1, at : at + HM, :] = value
            taps[0, at + 1 : at + 1 + HM, :] = value
            taps[2, at - 1 : at - 1 + HM, :] = value
        for at, rows, raw_left, raw_right in rims:
            from_left = jnp.where(t > 0, act(raw_left), 0.0)
            from_right = jnp.where(t < T - 1, act(raw_right), 0.0)
            taps[0, pl.ds(at, rows, stride=W), :] = from_left
            taps[2, pl.ds(at + W - 1, rows, stride=W), :] = from_right
        zero = jnp.zeros((W, LANES), F32)
        tail = jnp.zeros((taps.shape[1] - W - M, LANES), F32)
        for b in range(3):
            taps[b, 0:W, :] = zero
            taps[b, W + M :, :] = tail

    def first_remote():
        parts = []
        rims = []
        for dt in range(1, T):
            peer = lax.rem(t + dt, T)
            for j in range(S):
                rim_copy(dt, j, False).wait_recv()
                parts.append(
                    (
                        rim_in[peer, j, 2 * RE : 2 * RE + 1, :],
                        rim_in[peer, j, 2 * RE + 1 : 2 * RE + 2, :],
                        TILE,
                    )
                )
        for j in range(S):
            rims.append(
                (W + j * TILE, R, rim_in[left, j, RE : RE + R, :], rim_in[right, j, 0:R, :])
            )
        return parts, rims

    def later_remote(k, incoming):
        for copy in incoming:
            copy.wait_recv()
        parts = []
        rims = []
        for dt in range(1, T):
            peer = lax.rem(t + dt, T)
            for cc in range(C):
                parts.append(
                    (
                        msg_in[k, peer, cc, 2 * pad_edge : 2 * pad_edge + 1, :],
                        msg_in[k, peer, cc, 2 * pad_edge + 1 : 2 * pad_edge + 2, :],
                        HM,
                    )
                )
        for h in range(C):
            rims.append(
                (
                    W + h * HM,
                    HR,
                    msg_in[k, left, h, pad_edge : pad_edge + edge, :],
                    msg_in[k, right, h, 0:edge, :],
                )
            )
        return parts, rims

    def operand(start, rows):
        pairs = []
        for a in range(3):
            for b in range(3):
                pairs.append(split_pair(taps[b, start + a * W : start + a * W + rows, :]))
        return jnp.concatenate(
            [v for pair in pairs for v in pair] + [pair[0] for pair in pairs], axis=1
        )

    def piece_copy(k, i, h):
        block = c * BH + i
        return block, pltpu.make_async_remote_copy(
            src_ref=piece.at[k, i, h],
            dst_ref=piece_in.at[k, s],
            send_sem=p_ssem.at[k, i, h],
            recv_sem=p_rsem.at[k, s],
            device_id={"space": block, "chan": h},
            device_id_type=MESH,
        )

    def conv_send(k, mat):
        for h in range(2):
            part = jnp.dot(operand(h * HM, HM), mat[...], preferred_element_type=F32)
            for i in range(BH):
                pack(piece.at[k, i, h], part[:, i * LANES : (i + 1) * LANES], PM)
                block, copy = piece_copy(k, i, h)
                away = jnp.logical_or(block != s, c != h)

                @pl.when(away)
                def _():
                    copy.start()

                @pl.when(jnp.logical_not(away))
                def _():
                    piece_in[k, s] = piece[k, i, h]

    def conv_receive(k, full, extra):
        holder = s // BH
        for step in range(S):
            source = lax.rem(s + step, S)
            arrival = pltpu.make_async_remote_copy(
                src_ref=piece.at[k, 0, 0],
                dst_ref=piece_in.at[k, source],
                send_sem=p_ssem.at[k, 0, 0],
                recv_sem=p_rsem.at[k, source],
                device_id={"space": source, "chan": holder},
                device_id_type=MESH,
            )
            if step == 0:

                @pl.when(holder != c)
                def _():
                    arrival.wait_recv()

            else:
                arrival.wait_recv()
        total = piece_in[k, 0]
        for j in range(1, S):
            total = total + piece_in[k, j]
        at = 0
        for value in unpack(total, HM):
            rows = pl.ds(pl.multiple_of(c * HM + at, 8), value.shape[0])
            full[rows, :] = value if extra is None else value + extra[rows, :]
            at += value.shape[0]

    def conv_drain(k):
        for h in range(2):
            for i in range(BH):
                block, copy = piece_copy(k, i, h)

                @pl.when(jnp.logical_or(block != s, c != h))
                def _():
                    copy.wait_send()

    for load in loads[1:4]:
        load.wait()
    prepare(w1_raw, w1_mat)
    for step in range(1, S):
        a_copy(step, False).wait_recv()
        a_forward(step, c).start()
    for step in range(1, S):
        a_forward(step, other).wait_recv()
        source = lax.rem(s + step, S)
        at = 0
        for value in unpack(a_in[source], TILE):
            start = pl.multiple_of(source * TILE + at, 8)
            feat_all[pl.ds(start, value.shape[0]), :] = value
            at += value.shape[0]
    parts, rims = first_remote()
    activate(feat_all, parts, rims, pick_block(gain1), pick_block(shift1))
    conv_send(0, w1_mat)

    for load in loads[4:]:
        load.wait()
    prepare(w2_raw, w2_mat)
    for tap in range(9):
        high, low = split_pair(padded(head_w[tap], LANES))
        for place, value in ((2 * tap, high), (2 * tap + 1, high), (18 + tap, low)):
            wh_mat[:, place * LANES : (place + 1) * LANES] = value
    for first, mat in ((0, wn_mat), (4 * (Z + 4), wc_mat)):
        for b in range(2):
            for a in range(2):
                at = (b * 2 + a) * Z
                for n in range(strips):
                    high, low = split_pair(pw_raw[n, pl.ds(first + a * 2 + b, Z, stride=4), :])
                    lanes = slice(n * LANES, (n + 1) * LANES)
                    mat[at : at + Z, lanes] = high
                    mat[4 * Z + at : 4 * Z + at + Z, lanes] = high
                    mat[8 * Z + at : 8 * Z + at + Z, lanes] = low
    mark_sum = jnp.concatenate(
        [
            jnp.sum(pw_raw[n, 4 * Z : 4 * (Z + 4), :], axis=0, keepdims=True)
            for n in range(strips)
        ],
        axis=1,
    )

    PR, PC, PP = dims["PR"], dims["PC"], dims["PP"]
    FULLW = W * T
    cells[...] = jnp.zeros(cells.shape, F32)
    patch[...] = jnp.zeros(patch.shape, F32)

    def patches_of_cells():
        turned[...] = cells[...].T
        for b in range(2):
            picked = turned[pl.ds(b, PC, stride=2), :]
            for p in range(PR):
                patch[p * PP : p * PP + PC, b * 2 * Z : (b + 1) * 2 * Z] = picked[
                    :, p * 2 * Z : (p + 1) * 2 * Z
                ]
        high, low = split_pair(patch[:, 0 : 4 * Z])
        return jnp.concatenate([high, low, high], axis=1)

    for f in range(FR):
        for i in range(R):
            cells[i * Z : (i + 1) * Z, 0:FULLW] = noisy[f, i]
        got = jnp.dot(patches_of_cells(), wn_mat[...], preferred_element_type=F32)
        opening = (t * FR + f) == 0
        base[f] = got + patch_b[...].reshape(1, -1) + jnp.where(opening, mark_sum, 0.0)

    conv_receive(0, conv_all.at[0], None)
    sib1 = sibling(0, conv_all.at[0], c)
    sib1.start()
    out2, in2 = exchange(0, conv_all.at[0])
    sibling(0, conv_all.at[0], other).wait_recv()
    parts, rims = later_remote(0, in2)
    activate(conv_all.at[0], parts, rims, pick_block(gain2), pick_block(shift2))
    conv_send(1, w2_mat)

    conv_receive(1, conv_all.at[1], feat_all)
    sib2 = sibling(1, conv_all.at[1], c)
    sib2.start()
    out3, in3 = exchange(1, conv_all.at[1])
    sibling(1, conv_all.at[1], other).wait_recv()
    parts, rims = later_remote(1, in3)
    activate(conv_all.at[1], parts, rims, pick_block(gain3), pick_block(shift3))

    def lat_copy(dest_s, dest_t, dest_c, slot_s, slot_t, slot_c):
        return pltpu.make_async_remote_copy(
            src_ref=lat_send.at[dest_s],
            dst_ref=lat_in.at[slot_t, slot_c, slot_s],
            send_sem=l_ssem.at[dest_t, dest_c, dest_s],
            recv_sem=l_rsem.at[slot_t, slot_c, slot_s],
            device_id={"space": dest_s, "tm": dest_t, "chan": dest_c},
            device_id_type=MESH,
        )

    bias_row = jnp.broadcast_to(head_b[...].reshape(1, ZH), (ZH, ZH))
    diagonal = lax.broadcasted_iota(jnp.int32, (ZH, ZH), 0) == lax.broadcasted_iota(
        jnp.int32, (ZH, ZH), 1
    )
    bias = jnp.sum(jnp.where(diagonal & (s == 0), bias_row, 0.0), axis=1, keepdims=True)
    for j in range(S):
        part = lax.dot_general(
            wh_mat[...],
            operand(j * TILE, LANES),
            (((1,), (1,)), ((), ())),
            preferred_element_type=F32,
        )
        lat_send[j] = part + bias
    lat_in[t, c, s] = lat_send[s]
    lat_out = []
    lat_arrive = []
    for ds in reversed(range(S)):
        for dt in range(T):
            for dc in range(C):
                if ds or dt or dc:
                    ps = lax.rem(s + ds, S)
                    pt = lax.rem(t + dt, T)
                    pc = lax.rem(c + dc, C)
                    copy = lat_copy(ps, pt, pc, s, t, c)
                    copy.start()
                    lat_out.append(copy)
                    lat_arrive.append(lat_copy(ps, pt, pc, ps, pt, pc))

    conv_drain(0)
    conv_drain(1)
    for copy in out2 + out3 + [sib1, sib2]:
        copy.wait_send()
    for step in range(1, S):
        a_copy(step, True).wait_send()
        a_forward(step, c).wait_send()
    for dt in range(1, T):
        for j in range(S):
            rim_copy(dt, j, True).wait_send()

    for copy in lat_arrive:
        copy.wait_recv()

    def half_latent(tt, cc):
        total = lat_in[tt, cc, 0]
        for j in range(1, S):
            total = total + lat_in[tt, cc, j]
        return total

    for cc in range(C):
        value = half_latent(t, cc)
        for r in range(R):
            latent[r, cc * ZH : (cc + 1) * ZH, :] = value[:, r * W : (r + 1) * W]
    for f in range(FR):
        cells[...] = jnp.zeros(cells.shape, F32)
        opening = (t * FR + f) == 0
        for tt in range(T):
            for cc in range(C):
                value = half_latent(tt, cc)
                for i in range(R):
                    at = i * Z + cc * ZH
                    cells[at : at + ZH, tt * W : (tt + 1) * W] = value[:, i * W : (i + 1) * W]
        for i in range(R):
            rows = slice(i * Z, (i + 1) * Z)
            cells[rows, 0:FULLW] = jnp.where(opening, cells[rows, 0:FULLW], later[f, i])
        got = base[f] + jnp.dot(patches_of_cells(), wc_mat[...], preferred_element_type=F32)
        for p in range(PR):
            tokens[p, :, f, :] = got[p * PP : p * PP + PC, :]
    for copy in lat_out:
        copy.wait_send()


def up(value, unit):
    return -(-value // unit) * unit


def packed_rows(rows, width, unit):
    free = LANES - width
    if free <= 0 or width % free or rows % 8:
        return rows
    main = up(-(-rows * width // LANES), unit)
    fits = main < rows and (rows - main) * (width // free) <= main
    return main if fits else rows


def plan(mesh_shape, features, noisy_latents, patch_weight):
    S, T, C = mesh_shape["space"], mesh_shape["tm"], mesh_shape["chan"]
    R, W, CH = features.shape
    FR, Z = noisy_latents.shape[:2]
    dims = dict(S=S, T=T, C=C, R=R, W=W, CH=CH, Z=Z, FR=FR)
    H = S * R
    dims["EDGE"] = up(H // 2, 8)
    dims["PR"], dims["PC"] = R // 2, W * T // 2
    dims["PP"] = up(W * T // 2, 8)
    dims["N"] = patch_weight.shape[1]
    CB = CH // S
    dims["AM"], dims["PM"] = packed_rows(R * W, CB, 16), packed_rows(H * W // 2, CB, 8)
    dims["RE"] = up(R, 8)
    fits = (
        C == 2
        and T > 1
        and S % C == 0
        and CH % S == 0
        and CH // S <= LANES
        and (CH // S) % (CH // NGROUP) == 0
        and (R * W) % 8 == 0
        and (H * W // 2) % 8 == 0
        and H % 2 == 0
        and dims["AM"] % 16 == 0
        and dims["PM"] % 8 == 0
        and R * W <= LANES
        and R * Z <= LANES
        and W * T <= LANES
        and 4 * Z <= LANES
        and dims["N"] % LANES == 0
        and H * W * LANES * 4 <= 2**19
    )
    return dims if fits else None


def fused(dims, args):
    S, T, C = dims["S"], dims["T"], dims["C"]
    R, W, CH = dims["R"], dims["W"], dims["CH"]
    Z, FR, N, EDGE = dims["Z"], dims["FR"], dims["N"], dims["EDGE"]
    CB, NH = CH // S, CH // C
    BH = NH // CB
    M = S * R * W
    MR = 2 * EDGE + 8
    (f, g1, s1, w1, g2, s2, w2, g3, s3, hw, hb, noisy, later, pw, pb) = args
    flat = lambda v: v.reshape((9,) + v.shape[2:])
    by_row = lambda v: jnp.transpose(v, (0, 2, 1, 3))
    operands = (
        f, g1, s1, flat(w1), g2, s2, flat(w2), g3, s3,
        flat(jnp.transpose(hw, (0, 1, 3, 2))), hb, by_row(noisy), by_row(later), pw, pb,
    )
    vmem = pl.BlockSpec(memory_space=pltpu.VMEM)
    in_specs = [pl.BlockSpec(memory_space=pl.ANY)] * 15
    dma = pltpu.SemaphoreType.DMA
    big = lambda n: pltpu.VMEM((27 * LANES, n), BF16)
    scratch = [
        pltpu.VMEM(operands[k].shape, F32) for k in (0, 1, 2, 4, 5, 7, 8, 9, 10, 11, 12, 14)
    ] + [
        pltpu.VMEM((9, CB, NH), F32),
        pltpu.VMEM((9, CB, NH), F32),
        pltpu.VMEM((N // LANES, pw.shape[0], LANES), F32),
        big(BH * LANES),
        big(BH * LANES),
        pltpu.VMEM((Z // C, 27 * LANES), BF16),
        pltpu.VMEM((12 * Z, N), BF16),
        pltpu.VMEM((12 * Z, N), BF16),
        pltpu.VMEM((FR, dims["PR"] * dims["PP"], N), F32),
        pltpu.VMEM((S, R * W, LANES), F32),
        pltpu.VMEM((S, dims["AM"], LANES), F32),
        pltpu.VMEM((S, dims["AM"], LANES), F32),
        pltpu.VMEM((S, 2 * dims["RE"] + 8, LANES), F32),
        pltpu.VMEM((T, S, 2 * dims["RE"] + 8, LANES), F32),
        pltpu.VMEM((M, LANES), F32),
        pltpu.VMEM((2, M, LANES), F32),
        pltpu.VMEM((3, up(M + 2 * W + LANES, 8), LANES), F32),
        pltpu.VMEM((2, MR, LANES), F32),
        pltpu.VMEM((2, T, C, MR, LANES), F32),
        pltpu.VMEM((2, BH, 2, dims["PM"], LANES), F32),
        pltpu.VMEM((2, S, dims["PM"], LANES), F32),
        pltpu.VMEM((S, Z // C, LANES), F32),
        pltpu.VMEM((T, C, S, Z // C, LANES), F32),
        pltpu.VMEM((LANES, LANES), F32),
        pltpu.VMEM((LANES, LANES), F32),
        pltpu.VMEM((dims["PR"] * dims["PP"], LANES), F32),
        dma((14 + N // LANES,)),
        dma((S,)),
        dma((S,)),
        dma((S,)),
        dma((S,)),
        dma((T, S)),
        dma((T, S)),
        dma((2, T, C)),
        dma((2, T, C)),
        dma((2,)),
        dma((2,)),
        dma((2, BH, 2)),
        dma((2, S)),
        dma((T, C, S)),
        dma((T, C, S)),
    ]
    tokens, latent = pl.pallas_call(
        functools.partial(fused_kernel, dims),
        out_shape=(
            jax.ShapeDtypeStruct((dims["PR"], dims["PC"], FR, N), F32),
            jax.ShapeDtypeStruct((R, Z, W), F32),
        ),
        in_specs=in_specs,
        out_specs=(vmem, vmem),
        scratch_shapes=scratch,
        compiler_params=pltpu.CompilerParams(
            collective_id=0, has_side_effects=True, vmem_limit_bytes=60 * 2**20
        ),
        name="fused_block",
    )(*operands)
    return jnp.transpose(tokens, (2, 0, 1, 3)), jnp.transpose(latent, (0, 2, 1))


def solution(mesh):
    shape = dict(mesh.shape)

    def step(*args):
        dims = plan(shape, args[0], args[11], args[13])
        return on_device(*args) if dims is None else fused(dims, args)

    return jax.shard_map(
        step,
        mesh=mesh,
        in_specs=(
            P(("groups", "space"), "tm", None),
            P(),
            P(),
            P(None, None, "space", "chan"),
            P(),
            P(),
            P(None, None, "space", "chan"),
            P(),
            P(),
            P(None, None, "space", "chan"),
            P("chan"),
            P(("groups", "tm"), None, "space", None),
            P(("groups", "tm"), None, "space", None),
            P(None, "chan"),
            P("chan"),
        ),
        out_specs=(P(("groups", "tm"), "space", None, "chan"), P(("groups", "space"), "tm", None)),
        check_vma=False,
    )
```

```python
import functools

import jax
import jax.numpy as jnp
from jax import lax
from jax.experimental import pallas as pl
from jax.experimental.pallas import tpu as pltpu
from jax.sharding import PartitionSpec as P

NGROUP = 32


EPSILON = 1e-06
HIGHEST = lax.Precision.HIGHEST


def padded_2(cells, sides, width):
    for axis, dim in sides:
        count = lax.axis_size(axis)
        ends = count - 1
        head = lax.slice_in_dim(cells, 0, width, axis=dim)
        tail = lax.slice_in_dim(cells, cells.shape[dim] - width, cells.shape[dim], axis=dim)
        cells = jnp.concatenate(
            [
                lax.ppermute(tail, axis, [(i, (i + 1) % count) for i in range(ends)]),
                cells,
                lax.ppermute(head, axis, [((i + 1) % count, i) for i in range(ends)]),
            ],
            axis=dim,
        )
    return cells


def group_stats(inner, count_all):
    grouped = inner.reshape(-1, NGROUP, inner.shape[-1] // NGROUP)
    totals, squares = lax.psum(
        (jnp.sum(grouped, axis=(0, 2)), jnp.sum(grouped * grouped, axis=(0, 2))), ("space", "tm")
    )
    center = totals / count_all
    spread = squares / count_all - center * center
    return (center, lax.rsqrt(spread + EPSILON))


def normalize_act(values, stats, gain, shift):
    center, inverse = stats
    grouped = values.reshape(values.shape[:-1] + (NGROUP, values.shape[-1] // NGROUP))
    scaled = (grouped - center[:, None]) * inverse[:, None]
    return jax.nn.silu(scaled.reshape(values.shape) * gain + shift)


def tap_columns(padded, rows_out, cols_out):
    shifted = [
        padded[row_tap : row_tap + rows_out, col_tap : col_tap + cols_out, :]
        for row_tap in range(3)
        for col_tap in range(3)
    ]
    return jnp.stack(shifted, axis=2).reshape(rows_out * cols_out, 9, padded.shape[-1])


def add_taps(columns, piece):
    depth = piece.shape[2]
    picked = columns.reshape(columns.shape[0], 9 * depth)
    return jnp.dot(
        picked,
        piece.reshape(9 * depth, piece.shape[3]),
        precision=HIGHEST,
        preferred_element_type=jnp.float32,
    )


def wide_conv(padded, weight, rows_out, cols_out):
    columns = tap_columns(padded, rows_out, cols_out)
    summed = add_taps(columns, lax.all_gather(weight, "space", axis=2, tiled=True))
    return lax.all_gather(summed.reshape(rows_out, cols_out, -1), "chan", axis=2, tiled=True)


def border_rim(values):
    return padded_2(values, (("space", 0), ("tm", 1)), 1)


def on_device(
    features,
    norm1_gain,
    norm1_shift,
    conv1_weight,
    norm2_gain,
    norm2_shift,
    conv2_weight,
    head_gain,
    head_shift,
    head_weight,
    head_bias,
    noisy_latents,
    later_cond,
    patch_weight,
    patch_bias,
):
    tile_rows = features.shape[0]
    tile_cols = features.shape[1]
    count_all = float(
        tile_rows
        * tile_cols
        * lax.axis_size("space")
        * lax.axis_size("tm")
        * (features.shape[2] // NGROUP)
    )
    first_stats = group_stats(features, count_all)
    active = normalize_act(features, first_stats, norm1_gain, norm1_shift)
    first_conv = wide_conv(border_rim(active), conv1_weight, tile_rows, tile_cols)
    second_stats = group_stats(first_conv, count_all)
    second_act = normalize_act(first_conv, second_stats, norm2_gain, norm2_shift)
    second_conv = wide_conv(border_rim(second_act), conv2_weight, tile_rows, tile_cols)
    hidden = features + second_conv
    head_stats = group_stats(hidden, count_all)
    head_act = normalize_act(hidden, head_stats, head_gain, head_shift)
    head_pad = padded_2(head_act, (("space", 0), ("tm", 1)), 1)
    head_columns = tap_columns(head_pad, tile_rows, tile_cols)
    latent_part = (
        add_taps(head_columns, lax.all_gather(head_weight, "space", axis=2, tiled=True)) + head_bias
    )
    image_latent = lax.all_gather(
        latent_part.reshape(tile_rows, tile_cols, -1), "chan", axis=2, tiled=True
    )
    latent_row = lax.all_gather(image_latent, "tm", axis=1, tiled=True)
    frame_count = noisy_latents.shape[0]
    full_width = noisy_latents.shape[3]
    frame_ids = lax.axis_index("tm") * frame_count + jnp.arange(frame_count)
    opening = frame_ids == 0
    condition = jnp.where(
        opening[:, None, None, None], jnp.transpose(latent_row, (2, 0, 1))[None], later_cond
    )
    marks = jnp.broadcast_to(
        opening.astype(jnp.float32)[:, None, None, None], (frame_count, 4, tile_rows, full_width)
    )
    stacked = jnp.concatenate([noisy_latents, marks, condition], axis=1)
    channel_count = stacked.shape[1]
    patches = (
        stacked.reshape(frame_count, channel_count, tile_rows // 2, 2, full_width // 2, 2)
        .transpose(0, 2, 4, 1, 3, 5)
        .reshape(-1, channel_count * 4)
    )
    tokens = (
        jnp.dot(patches, patch_weight, precision=HIGHEST, preferred_element_type=jnp.float32)
        + patch_bias
    )
    return (tokens.reshape(frame_count, tile_rows // 2, full_width // 2, -1), image_latent)


MESH = pl.DeviceIdType.MESH
LANES = 128
BF16 = jnp.bfloat16
F32 = jnp.float32


def split_pair(values):
    high = values.astype(BF16)
    return high, (values - high.astype(F32)).astype(BF16)


def split_columns(values):
    high, low = split_pair(values)
    return jnp.concatenate([high, low, high], axis=1)


def finish_kernel(dims, patch, base, wc, latent_in, tokens, latent):
    PC, PP, Z = dims["PC"], dims["PP"], dims["Z"]
    for f in range(dims["FR"]):
        lhs = split_columns(patch[f, :, 0 : 4 * Z])
        got = base[f] + jnp.dot(lhs, wc[...], preferred_element_type=F32)
        for p in range(dims["PR"]):
            tokens[p, :, f, :] = got[p * PP : p * PP + PC, :]
    latent[...] = latent_in[...]


def fused_kernel(
    dims,
    feat_hbm,
    gain1_hbm,
    shift1_hbm,
    w1_hbm,
    gain2_hbm,
    shift2_hbm,
    w2_hbm,
    gain3_hbm,
    shift3_hbm,
    head_w_hbm,
    head_b_hbm,
    noisy_hbm,
    later_hbm,
    pw_hbm,
    patch_b_hbm,
    patch_out,
    base_out,
    wc_out,
    latent,
    feat,
    gain1,
    shift1,
    gain2,
    shift2,
    gain3,
    shift3,
    head_w,
    head_b,
    noisy,
    later,
    patch_b,
    w1_raw,
    w2_raw,
    pw_raw,
    w1_mat,
    w2_mat,
    wh_mat,
    mixed,
    wn_mat,
    wc_mat,
    base,
    a_send,
    a_pack,
    a_in,
    rim,
    rim_in,
    feat_all,
    conv_all,
    taps,
    msg,
    msg_in,
    piece,
    piece_in,
    lat_send,
    lat_in,
    cells,
    turned,
    patch,
    load_sem,
    a_ssem,
    a_rsem,
    f_ssem,
    f_rsem,
    r_ssem,
    r_rsem,
    m_ssem,
    m_rsem,
    sib_ssem,
    sib_rsem,
    p_ssem,
    p_rsem,
    l_ssem,
    l_rsem,
):
    S, T, C = dims["S"], dims["T"], dims["C"]
    R, W, CH = dims["R"], dims["W"], dims["CH"]
    Z, FR = dims["Z"], dims["FR"]
    CB = CH // S
    NH = CH // C
    BH = NH // CB
    H = S * R
    M = H * W
    HM = M // 2
    HR = H // 2
    TILE = R * W
    per_group = CH // NGROUP
    ZH = Z // C
    s = lax.axis_index("space")
    t = lax.axis_index("tm")
    c = lax.axis_index("chan")
    other = 1 - c

    early = (
        (feat_hbm, feat), (w1_hbm, w1_raw), (gain1_hbm, gain1), (shift1_hbm, shift1),
        (w2_hbm, w2_raw), (gain2_hbm, gain2), (shift2_hbm, shift2),
        (gain3_hbm, gain3), (shift3_hbm, shift3), (head_w_hbm, head_w), (head_b_hbm, head_b),
        (noisy_hbm, noisy), (later_hbm, later), (patch_b_hbm, patch_b),
    )
    loads = [
        pltpu.make_async_copy(src, dst, load_sem.at[k]) for k, (src, dst) in enumerate(early)
    ]
    strips = pw_raw.shape[0]
    loads += [
        pltpu.make_async_copy(
            pw_hbm.at[:, n * LANES : (n + 1) * LANES], pw_raw.at[n], load_sem.at[len(early) + n]
        )
        for n in range(strips)
    ]
    for load in loads:
        load.start()

    barrier = pltpu.get_barrier_semaphore()
    for ds in range(S):
        for dt in range(T):
            for dc in range(C):
                if ds or dt or dc:
                    pl.semaphore_signal(
                        barrier,
                        inc=1,
                        device_id={
                            "space": lax.rem(s + ds, S),
                            "tm": lax.rem(t + dt, T),
                            "chan": lax.rem(c + dc, C),
                        },
                        device_id_type=MESH,
                    )

    def padded(values, width):
        rows = values.shape[0]
        if width == values.shape[1]:
            return values
        return jnp.concatenate([values, jnp.zeros((rows, width - values.shape[1]), values.dtype)], axis=1)

    loads[0].wait()
    for r in range(R):
        line = feat[r]
        for j in range(S):
            a_send[j, r * W : (r + 1) * W, :] = padded(line[:, j * CB : (j + 1) * CB], LANES)

    def pack(dst, value, main):
        rows = value.shape[0]
        dst[...] = value[0:main]
        rest = rows - main
        free = LANES - CB
        for j in range(CB // free if rest else 0):
            dst[j * rest : (j + 1) * rest, CB:LANES] = value[main:rows, j * free : (j + 1) * free]

    def unpack(value, rows):
        main = value.shape[0]
        rest = rows - main
        if not rest:
            return (value,)
        free = LANES - CB
        columns = [value[j * rest : (j + 1) * rest, CB:LANES] for j in range(CB // free)]
        return value, padded(jnp.concatenate(columns, axis=1), LANES)

    def channel_stats(values):
        total = jnp.sum(values, axis=0, keepdims=True)
        middle = total * (1.0 / values.shape[0])
        away = values - middle
        return total, jnp.sum(away * away, axis=0, keepdims=True)

    AM, PM, RE = dims["AM"], dims["PM"], dims["RE"]
    AH = AM // 2
    for j in range(S):
        pack(a_pack.at[j], a_send[j], AM)

    pl.semaphore_wait(barrier, S * T * C - 1)

    def a_copy(step, sent):
        peer = lax.rem(s + step, S)
        slot = s if sent else peer
        mine = pl.ds(pl.multiple_of(c * AH, 8), AH)
        return pltpu.make_async_remote_copy(
            src_ref=a_pack.at[peer, mine],
            dst_ref=a_in.at[slot, mine],
            send_sem=a_ssem.at[peer],
            recv_sem=a_rsem.at[slot],
            device_id={"space": peer},
            device_id_type=MESH,
        )

    def a_forward(step, half):
        source = lax.rem(s + step, S)
        rows = pl.ds(pl.multiple_of(half * AH, 8), AH)
        return pltpu.make_async_remote_copy(
            src_ref=a_in.at[source, rows],
            dst_ref=a_in.at[source, rows],
            send_sem=f_ssem.at[source],
            recv_sem=f_rsem.at[source],
            device_id={"chan": other},
            device_id_type=MESH,
        )

    def rim_copy(dt, j, sent):
        peer = lax.rem(t + dt, T)
        slot_t, slot_s = (t, s) if sent else (peer, j)
        return pltpu.make_async_remote_copy(
            src_ref=rim.at[j],
            dst_ref=rim_in.at[slot_t, slot_s],
            send_sem=r_ssem.at[peer, j],
            recv_sem=r_rsem.at[slot_t, slot_s],
            device_id={"space": j, "tm": peer},
            device_id_type=MESH,
        )

    for step in range(1, S):
        a_copy(step, True).start()
    for j in range(S):
        total, spread = channel_stats(a_send[j])
        rim[j, 0:R, :] = a_send[j, pl.ds(0, R, stride=W), :]
        rim[j, RE : RE + R, :] = a_send[j, pl.ds(W - 1, R, stride=W), :]
        rim[j, 2 * RE : 2 * RE + 1, :] = total
        rim[j, 2 * RE + 1 : 2 * RE + 2, :] = spread
    for dt in range(1, T):
        for j in range(S):
            rim_copy(dt, j, True).start()
    feat_all[pl.ds(pl.multiple_of(s * TILE, 8), TILE), :] = a_send[s]

    def pick_block(ref):
        row = ref[...].reshape(1, CH)
        out = jnp.zeros((1, CB), F32)
        for j in range(S):
            out = jnp.where(s == j, row[:, j * CB : (j + 1) * CB], out)
        return padded(out, LANES)

    row_id = lax.broadcasted_iota(jnp.int32, (LANES, LANES), 0)
    col_id = lax.broadcasted_iota(jnp.int32, (LANES, LANES), 1)
    same = ((row_id // per_group) == (col_id // per_group)) & (row_id < CB) & (col_id < CB)
    member = jnp.where(same, 1.0, 0.0).astype(F32)

    def group_sum(row):
        wide = jnp.broadcast_to(row, (8, LANES))
        return jnp.dot(wide, member, precision=HIGHEST, preferred_element_type=F32)[0:1]

    def prepare(raw, mat):
        gap = jnp.zeros((LANES - CB, BH * LANES), BF16) if CB < LANES else None
        for tap in range(9):
            w = raw[tap]
            wide = jnp.concatenate(
                [padded(w[:, i * CB : (i + 1) * CB], LANES) for i in range(BH)], axis=1
            )
            high, low = split_pair(wide)
            store_split(mat, tap, high, low, gap)

    def store_split(mat, tap, high, low, gap):
        for place, value in ((2 * tap, high), (2 * tap + 1, high), (18 + tap, low)):
            mat[place * LANES : place * LANES + CB, :] = value
            if gap is not None:
                mat[place * LANES + CB : (place + 1) * LANES, :] = gap

    edge = HR
    pad_edge = dims["EDGE"]

    def exchange(k, full):
        start = pl.multiple_of(c * HM, 8)
        total, spread = channel_stats(full[pl.ds(start, HM), :])
        msg[k, 0:edge, :] = full[pl.ds(start, HR, stride=W), :]
        msg[k, pad_edge : pad_edge + edge, :] = full[pl.ds(start + (W - 1), HR, stride=W), :]
        msg[k, 2 * pad_edge : 2 * pad_edge + 1, :] = total
        msg[k, 2 * pad_edge + 1 : 2 * pad_edge + 2, :] = spread

        def copies(slot_t, slot_c, peer_t, peer_c, dc):
            return pltpu.make_async_remote_copy(
                src_ref=msg.at[k],
                dst_ref=msg_in.at[k, slot_t, slot_c],
                send_sem=m_ssem.at[k, peer_t, peer_c],
                recv_sem=m_rsem.at[k, slot_t, slot_c],
                device_id={"tm": peer_t, "chan": peer_c},
                device_id_type=MESH,
            )

        outgoing = []
        incoming = []
        for dt in range(1, T):
            for dc in range(C):
                peer_t = lax.rem(t + dt, T)
                peer_c = lax.rem(c + dc, C)
                outgoing.append(copies(t, c, peer_t, peer_c, dc))
                incoming.append(copies(peer_t, peer_c, peer_t, peer_c, dc))
        for copy in outgoing:
            copy.start()
        return outgoing, incoming

    def sibling(k, full, mine):
        start = pl.multiple_of(mine * HM, 8)
        return pltpu.make_async_remote_copy(
            src_ref=full.at[pl.ds(start, HM)],
            dst_ref=full.at[pl.ds(start, HM)],
            send_sem=sib_ssem.at[k],
            recv_sem=sib_rsem.at[k],
            device_id={"chan": other},
            device_id_type=MESH,
        )

    left = lax.rem(t + T - 1, T)
    right = lax.rem(t + 1, T)

    def activate(full, remote, rims, gain, shift):
        parts = [channel_stats(full[h * HM : (h + 1) * HM, :]) + (HM,) for h in range(2)]
        parts += remote
        scale = 1.0 / float(per_group * M * T)
        total = parts[0][0]
        for part in parts[1:]:
            total = total + part[0]
        center = group_sum(total) * scale
        gathered = jnp.zeros((1, LANES), F32)
        for part_total, part_spread, count in parts:
            away = part_total * (1.0 / count) - center
            gathered = gathered + part_spread + away * away * float(count)
        inverse = lax.rsqrt(group_sum(gathered) * scale + EPSILON)
        multiply = inverse

        def act(values):
            u = (values - center) * multiply * gain + shift
            return u / (1.0 + jnp.exp(-u))

        for h in range(2):
            value = act(full[h * HM : (h + 1) * HM, :])
            at = W + h * HM
            taps[1, at : at + HM, :] = value
            taps[0, at + 1 : at + 1 + HM, :] = value
            taps[2, at - 1 : at - 1 + HM, :] = value
        for at, rows, raw_left, raw_right in rims:
            from_left = jnp.where(t > 0, act(raw_left), 0.0)
            from_right = jnp.where(t < T - 1, act(raw_right), 0.0)
            taps[0, pl.ds(at, rows, stride=W), :] = from_left
            taps[2, pl.ds(at + W - 1, rows, stride=W), :] = from_right
        zero = jnp.zeros((W, LANES), F32)
        tail = jnp.zeros((taps.shape[1] - W - M, LANES), F32)
        for b in range(3):
            taps[b, 0:W, :] = zero
            taps[b, W + M :, :] = tail

    def first_remote():
        parts = []
        rims = []
        for dt in range(1, T):
            peer = lax.rem(t + dt, T)
            for j in range(S):
                rim_copy(dt, j, False).wait_recv()
                parts.append(
                    (
                        rim_in[peer, j, 2 * RE : 2 * RE + 1, :],
                        rim_in[peer, j, 2 * RE + 1 : 2 * RE + 2, :],
                        TILE,
                    )
                )
        for j in range(S):
            rims.append(
                (W + j * TILE, R, rim_in[left, j, RE : RE + R, :], rim_in[right, j, 0:R, :])
            )
        return parts, rims

    def later_remote(k, incoming):
        for copy in incoming:
            copy.wait_recv()
        parts = []
        rims = []
        for dt in range(1, T):
            peer = lax.rem(t + dt, T)
            for cc in range(C):
                parts.append(
                    (
                        msg_in[k, peer, cc, 2 * pad_edge : 2 * pad_edge + 1, :],
                        msg_in[k, peer, cc, 2 * pad_edge + 1 : 2 * pad_edge + 2, :],
                        HM,
                    )
                )
        for h in range(C):
            rims.append(
                (
                    W + h * HM,
                    HR,
                    msg_in[k, left, h, pad_edge : pad_edge + edge, :],
                    msg_in[k, right, h, 0:edge, :],
                )
            )
        return parts, rims

    def operand(start, rows):
        pairs = []
        for a in range(3):
            for b in range(3):
                pairs.append(split_pair(taps[b, start + a * W : start + a * W + rows, :]))
        return jnp.concatenate(
            [v for pair in pairs for v in pair] + [pair[0] for pair in pairs], axis=1
        )

    def piece_copy(k, i, h):
        block = c * BH + i
        return block, pltpu.make_async_remote_copy(
            src_ref=piece.at[k, i, h],
            dst_ref=piece_in.at[k, s],
            send_sem=p_ssem.at[k, i, h],
            recv_sem=p_rsem.at[k, s],
            device_id={"space": block, "chan": h},
            device_id_type=MESH,
        )

    def conv_send(k, mat):
        for h in range(2):
            part = jnp.dot(operand(h * HM, HM), mat[...], preferred_element_type=F32)
            for i in range(BH):
                pack(piece.at[k, i, h], part[:, i * LANES : (i + 1) * LANES], PM)
                block, copy = piece_copy(k, i, h)
                away = jnp.logical_or(block != s, c != h)

                @pl.when(away)
                def _():
                    copy.start()

                @pl.when(jnp.logical_not(away))
                def _():
                    piece_in[k, s] = piece[k, i, h]

    def conv_receive(k, full, extra):
        holder = s // BH
        for step in range(S):
            source = lax.rem(s + step, S)
            arrival = pltpu.make_async_remote_copy(
                src_ref=piece.at[k, 0, 0],
                dst_ref=piece_in.at[k, source],
                send_sem=p_ssem.at[k, 0, 0],
                recv_sem=p_rsem.at[k, source],
                device_id={"space": source, "chan": holder},
                device_id_type=MESH,
            )
            if step == 0:

                @pl.when(holder != c)
                def _():
                    arrival.wait_recv()

            else:
                arrival.wait_recv()
        total = piece_in[k, 0]
        for j in range(1, S):
            total = total + piece_in[k, j]
        at = 0
        for value in unpack(total, HM):
            rows = pl.ds(pl.multiple_of(c * HM + at, 8), value.shape[0])
            full[rows, :] = value if extra is None else value + extra[rows, :]
            at += value.shape[0]

    def conv_drain(k):
        for h in range(2):
            for i in range(BH):
                block, copy = piece_copy(k, i, h)

                @pl.when(jnp.logical_or(block != s, c != h))
                def _():
                    copy.wait_send()

    for load in loads[1:4]:
        load.wait()
    prepare(w1_raw, w1_mat)
    for step in range(1, S):
        a_copy(step, False).wait_recv()
        a_forward(step, c).start()
    for step in range(1, S):
        a_forward(step, other).wait_recv()
        source = lax.rem(s + step, S)
        at = 0
        for value in unpack(a_in[source], TILE):
            start = pl.multiple_of(source * TILE + at, 8)
            feat_all[pl.ds(start, value.shape[0]), :] = value
            at += value.shape[0]
    parts, rims = first_remote()
    activate(feat_all, parts, rims, pick_block(gain1), pick_block(shift1))
    conv_send(0, w1_mat)

    for load in loads[4:]:
        load.wait()
    prepare(w2_raw, w2_mat)
    blank = jnp.zeros((LANES - 3 * ZH, LANES), F32)
    for b in range(3):
        rows = [padded(head_w[a * 3 + b], LANES) for a in range(3)] + [blank]
        high, low = split_pair(jnp.concatenate(rows, axis=0))
        for place, value in ((3 * b, high), (3 * b + 1, high), (3 * b + 2, low)):
            wh_mat[:, place * LANES : (place + 1) * LANES] = value
    for first, mat in ((0, wn_mat), (4 * (Z + 4), wc_mat)):
        for b in range(2):
            for a in range(2):
                at = (b * 2 + a) * Z
                for n in range(strips):
                    high, low = split_pair(pw_raw[n, pl.ds(first + a * 2 + b, Z, stride=4), :])
                    lanes = slice(n * LANES, (n + 1) * LANES)
                    mat[at : at + Z, lanes] = high
                    mat[4 * Z + at : 4 * Z + at + Z, lanes] = high
                    mat[8 * Z + at : 8 * Z + at + Z, lanes] = low
    mark_sum = jnp.concatenate(
        [
            jnp.sum(pw_raw[n, 4 * Z : 4 * (Z + 4), :], axis=0, keepdims=True)
            for n in range(strips)
        ],
        axis=1,
    )

    PR, PC, PP = dims["PR"], dims["PC"], dims["PP"]
    FULLW = W * T
    cells[...] = jnp.zeros(cells.shape, F32)
    patch[...] = jnp.zeros(patch.shape, F32)

    def build_patches():
        turned[...] = cells[...].T
        for b in range(2):
            picked = turned[pl.ds(b, PC, stride=2), :]
            for p in range(PR):
                patch[p * PP : p * PP + PC, b * 2 * Z : (b + 1) * 2 * Z] = picked[
                    :, p * 2 * Z : (p + 1) * 2 * Z
                ]

    for f in range(FR):
        for i in range(R):
            cells[i * Z : (i + 1) * Z, 0:FULLW] = noisy[f, i]
        build_patches()
        got = jnp.dot(split_columns(patch[:, 0 : 4 * Z]), wn_mat[...], preferred_element_type=F32)
        opening = (t * FR + f) == 0
        base[f] = got + patch_b[...].reshape(1, -1) + jnp.where(opening, mark_sum, 0.0)

    stores = [
        pltpu.make_async_copy(base, base_out, load_sem.at[len(early) + strips]),
        pltpu.make_async_copy(wc_mat, wc_out, load_sem.at[len(early) + strips + 1]),
    ]
    for store in stores:
        store.start()

    conv_receive(0, conv_all.at[0], None)
    sib1 = sibling(0, conv_all.at[0], c)
    sib1.start()
    out2, in2 = exchange(0, conv_all.at[0])
    sibling(0, conv_all.at[0], other).wait_recv()
    parts, rims = later_remote(0, in2)
    activate(conv_all.at[0], parts, rims, pick_block(gain2), pick_block(shift2))
    conv_send(1, w2_mat)

    conv_receive(1, conv_all.at[1], feat_all)
    sib2 = sibling(1, conv_all.at[1], c)
    sib2.start()
    out3, in3 = exchange(1, conv_all.at[1])
    sibling(1, conv_all.at[1], other).wait_recv()
    parts, rims = later_remote(1, in3)
    activate(conv_all.at[1], parts, rims, pick_block(gain3), pick_block(shift3))

    def lat_copy(dest_s, dest_t, dest_c, slot_s, slot_t, slot_c):
        return pltpu.make_async_remote_copy(
            src_ref=lat_send.at[dest_s],
            dst_ref=lat_in.at[slot_t, slot_c, slot_s],
            send_sem=l_ssem.at[dest_t, dest_c, dest_s],
            recv_sem=l_rsem.at[slot_t, slot_c, slot_s],
            device_id={"space": dest_s, "tm": dest_t, "chan": dest_c},
            device_id_type=MESH,
        )

    bias_row = jnp.broadcast_to(head_b[...].reshape(1, ZH), (ZH, ZH))
    diagonal = lax.broadcasted_iota(jnp.int32, (ZH, ZH), 0) == lax.broadcasted_iota(
        jnp.int32, (ZH, ZH), 1
    )
    bias = jnp.sum(jnp.where(diagonal & (s == 0), bias_row, 0.0), axis=1, keepdims=True)
    columns = []
    for b in range(3):
        high, low = split_pair(taps[b, 0 : mixed.shape[0], :])
        columns += [high, low, high]
    mixed[...] = lax.dot_general(
        jnp.concatenate(columns, axis=1),
        wh_mat[...],
        (((1,), (1,)), ((), ())),
        preferred_element_type=F32,
    )
    for j in range(S):
        shifted = [mixed[j * TILE + a * W : j * TILE + a * W + LANES, :] for a in range(3)]
        joined = jnp.where(
            col_id < ZH, shifted[0], jnp.where(col_id < 2 * ZH, shifted[1], shifted[2])
        ).T
        lat_send[j] = joined[0:ZH] + joined[ZH : 2 * ZH] + joined[2 * ZH : 3 * ZH] + bias
    lat_in[t, c, s] = lat_send[s]
    lat_out = []
    lat_arrive = []
    for ds in reversed(range(S)):
        for dt in range(T):
            for dc in range(C):
                if ds or dt or dc:
                    ps = lax.rem(s + ds, S)
                    pt = lax.rem(t + dt, T)
                    pc = lax.rem(c + dc, C)
                    copy = lat_copy(ps, pt, pc, s, t, c)
                    copy.start()
                    lat_out.append(copy)
                    lat_arrive.append(lat_copy(ps, pt, pc, ps, pt, pc))

    conv_drain(0)
    conv_drain(1)
    for copy in out2 + out3 + [sib1, sib2]:
        copy.wait_send()
    for step in range(1, S):
        a_copy(step, True).wait_send()
        a_forward(step, c).wait_send()
    for dt in range(1, T):
        for j in range(S):
            rim_copy(dt, j, True).wait_send()

    for copy in lat_arrive:
        copy.wait_recv()

    def half_latent(tt, cc):
        total = lat_in[tt, cc, 0]
        for j in range(1, S):
            total = total + lat_in[tt, cc, j]
        return total

    for cc in range(C):
        value = half_latent(t, cc)
        for r in range(R):
            latent[r, cc * ZH : (cc + 1) * ZH, :] = value[:, r * W : (r + 1) * W]
    for f in range(FR):
        cells[...] = jnp.zeros(cells.shape, F32)
        opening = (t * FR + f) == 0
        for tt in range(T):
            for cc in range(C):
                value = half_latent(tt, cc)
                for i in range(R):
                    at = i * Z + cc * ZH
                    cells[at : at + ZH, tt * W : (tt + 1) * W] = value[:, i * W : (i + 1) * W]
        for i in range(R):
            rows = slice(i * Z, (i + 1) * Z)
            cells[rows, 0:FULLW] = jnp.where(opening, cells[rows, 0:FULLW], later[f, i])
        build_patches()
        patch_out[f] = patch[...]
    for store in stores:
        store.wait()
    for copy in lat_out:
        copy.wait_send()


def up(value, unit):
    return -(-value // unit) * unit


def packed_rows(rows, width, unit):
    free = LANES - width
    if free <= 0 or width % free or rows % 8:
        return rows
    main = up(-(-rows * width // LANES), unit)
    fits = main < rows and (rows - main) * (width // free) <= main
    return main if fits else rows


def plan(mesh_shape, features, noisy_latents, patch_weight):
    S, T, C = mesh_shape["space"], mesh_shape["tm"], mesh_shape["chan"]
    R, W, CH = features.shape
    FR, Z = noisy_latents.shape[:2]
    dims = dict(S=S, T=T, C=C, R=R, W=W, CH=CH, Z=Z, FR=FR)
    H = S * R
    dims["EDGE"] = up(H // 2, 8)
    dims["PR"], dims["PC"] = R // 2, W * T // 2
    dims["PP"] = up(W * T // 2, 8)
    dims["N"] = patch_weight.shape[1]
    CB = CH // S
    dims["AM"], dims["PM"] = packed_rows(R * W, CB, 16), packed_rows(H * W // 2, CB, 8)
    dims["RE"] = up(R, 8)
    fits = (
        C == 2
        and T > 1
        and S % C == 0
        and CH % S == 0
        and CH // S <= LANES
        and (CH // S) % (CH // NGROUP) == 0
        and (R * W) % 8 == 0
        and (H * W // 2) % 8 == 0
        and H % 2 == 0
        and dims["AM"] % 16 == 0
        and dims["PM"] % 8 == 0
        and R * W <= LANES
        and R * Z <= LANES
        and W * T <= LANES
        and 4 * Z <= LANES
        and dims["N"] % LANES == 0
        and H * W * LANES * 4 <= 2**19
    )
    return dims if fits else None


def fused(dims, args):
    S, T, C = dims["S"], dims["T"], dims["C"]
    R, W, CH = dims["R"], dims["W"], dims["CH"]
    Z, FR, N, EDGE = dims["Z"], dims["FR"], dims["N"], dims["EDGE"]
    CB, NH = CH // S, CH // C
    BH = NH // CB
    M = S * R * W
    MR = 2 * EDGE + 8
    (f, g1, s1, w1, g2, s2, w2, g3, s3, hw, hb, noisy, later, pw, pb) = args
    flat = lambda v: v.reshape((9,) + v.shape[2:])
    by_row = lambda v: jnp.transpose(v, (0, 2, 1, 3))
    operands = (
        f, g1, s1, flat(w1), g2, s2, flat(w2), g3, s3,
        flat(jnp.transpose(hw, (0, 1, 3, 2))), hb, by_row(noisy), by_row(later), pw, pb,
    )
    vmem = pl.BlockSpec(memory_space=pltpu.VMEM)
    in_specs = [pl.BlockSpec(memory_space=pl.ANY)] * 15
    dma = pltpu.SemaphoreType.DMA
    big = lambda n: pltpu.VMEM((27 * LANES, n), BF16)
    scratch = [
        pltpu.VMEM(operands[k].shape, F32) for k in (0, 1, 2, 4, 5, 7, 8, 9, 10, 11, 12, 14)
    ] + [
        pltpu.VMEM((9, CB, NH), F32),
        pltpu.VMEM((9, CB, NH), F32),
        pltpu.VMEM((N // LANES, pw.shape[0], LANES), F32),
        big(BH * LANES),
        big(BH * LANES),
        pltpu.VMEM((LANES, 9 * LANES), BF16),
        pltpu.VMEM((up((S - 1) * R * W + 2 * W + LANES, 16), LANES), F32),
        pltpu.VMEM((12 * Z, N), BF16),
        pltpu.VMEM((12 * Z, N), BF16),
        pltpu.VMEM((FR, dims["PR"] * dims["PP"], N), F32),
        pltpu.VMEM((S, R * W, LANES), F32),
        pltpu.VMEM((S, dims["AM"], LANES), F32),
        pltpu.VMEM((S, dims["AM"], LANES), F32),
        pltpu.VMEM((S, 2 * dims["RE"] + 8, LANES), F32),
        pltpu.VMEM((T, S, 2 * dims["RE"] + 8, LANES), F32),
        pltpu.VMEM((M, LANES), F32),
        pltpu.VMEM((2, M, LANES), F32),
        pltpu.VMEM((3, up(M + 2 * W + LANES, 8), LANES), F32),
        pltpu.VMEM((2, MR, LANES), F32),
        pltpu.VMEM((2, T, C, MR, LANES), F32),
        pltpu.VMEM((2, BH, 2, dims["PM"], LANES), F32),
        pltpu.VMEM((2, S, dims["PM"], LANES), F32),
        pltpu.VMEM((S, Z // C, LANES), F32),
        pltpu.VMEM((T, C, S, Z // C, LANES), F32),
        pltpu.VMEM((LANES, LANES), F32),
        pltpu.VMEM((LANES, LANES), F32),
        pltpu.VMEM((dims["PR"] * dims["PP"], LANES), F32),
        dma((16 + N // LANES,)),
        dma((S,)),
        dma((S,)),
        dma((S,)),
        dma((S,)),
        dma((T, S)),
        dma((T, S)),
        dma((2, T, C)),
        dma((2, T, C)),
        dma((2,)),
        dma((2,)),
        dma((2, BH, 2)),
        dma((2, S)),
        dma((T, C, S)),
        dma((T, C, S)),
    ]
    PR, PC, PP = dims["PR"], dims["PC"], dims["PP"]
    far = pl.BlockSpec(memory_space=pl.ANY)
    patch, base, wc, latent = pl.pallas_call(
        functools.partial(fused_kernel, dims),
        out_shape=(
            jax.ShapeDtypeStruct((FR, PR * PP, LANES), F32),
            jax.ShapeDtypeStruct((FR, PR * PP, N), F32),
            jax.ShapeDtypeStruct((12 * Z, N), BF16),
            jax.ShapeDtypeStruct((R, Z, W), F32),
        ),
        in_specs=in_specs,
        out_specs=(vmem, far, far, vmem),
        scratch_shapes=scratch,
        compiler_params=pltpu.CompilerParams(
            collective_id=0, has_side_effects=True, vmem_limit_bytes=60 * 2**20
        ),
        name="fused_block",
    )(*operands)
    NB = N // 4 if N % (4 * LANES) == 0 else N
    whole = lambda shape: pl.BlockSpec(shape, lambda n: (0,) * len(shape))
    tokens, latent = pl.pallas_call(
        functools.partial(finish_kernel, dims),
        grid=(N // NB,),
        out_shape=(
            jax.ShapeDtypeStruct((PR, PC, FR, N), F32),
            jax.ShapeDtypeStruct((R, Z, W), F32),
        ),
        in_specs=[
            whole((FR, PR * PP, LANES)),
            pl.BlockSpec((FR, PR * PP, NB), lambda n: (0, 0, n)),
            pl.BlockSpec((12 * Z, NB), lambda n: (0, n)),
            whole((R, Z, W)),
        ],
        out_specs=(pl.BlockSpec((PR, PC, FR, NB), lambda n: (0, 0, 0, n)), whole((R, Z, W))),
        name="finish_tokens",
    )(patch, base, wc, latent)
    return jnp.transpose(tokens, (2, 0, 1, 3)), jnp.transpose(latent, (0, 2, 1))


def solution(mesh):
    shape = dict(mesh.shape)

    def step(*args):
        dims = plan(shape, args[0], args[11], args[13])
        return on_device(*args) if dims is None else fused(dims, args)

    return jax.shard_map(
        step,
        mesh=mesh,
        in_specs=(
            P(("groups", "space"), "tm", None),
            P(),
            P(),
            P(None, None, "space", "chan"),
            P(),
            P(),
            P(None, None, "space", "chan"),
            P(),
            P(),
            P(None, None, "space", "chan"),
            P("chan"),
            P(("groups", "tm"), None, "space", None),
            P(("groups", "tm"), None, "space", None),
            P(None, "chan"),
            P("chan"),
        ),
        out_specs=(P(("groups", "tm"), "space", None, "chan"), P(("groups", "space"), "tm", None)),
        check_vma=False,
    )
```
